32 devices in a mesh: depth: 4 (over y, core), image: 8 (over z, x).
Axes of the slice: x: 2, y: 2, z: 4, core: 2. Of those that a mesh axis runs over, the one named last changes fastest.
Arguments:
- populations: float32 [19, 128, 128, 128], P(None, 'depth', 'image'), may hold values from 0 to 0.4, as said below
- transfer: float32 [8, 5, 8], P('image'), may hold values from 0.1 to 1
- direction: int32 [8], P('image'), may hold values from 0 to 1
Outputs:
- final_populations: float32 [19, 128, 128, 128], P(None, 'depth', 'image')
- vorticity: bfloat16 [128, 128, 128], P('depth', 'image')
- images: float32 [8, 4, 128, 128], P('image', None, 'depth')
The draws below stay inside these ranges and needn't reach their ends.
Inputs may be any that keep to these rules, and one draw needn't show every extreme that they name: `populations`: each population is positive, its lattice weight times a density near one with a perturbation by a rough flow of small speed. `direction`: 0 views from the side of small x, 1 from the side of large x.
All inputs are finite; a program needn't handle non-finite values.
Results may differ from the reference program's by a relative error of at most 0.001.
Values may be sent and summed in bfloat16 or wider, within the bound.
A program may use at most 128 MiB of HBM per device.

```python
import jax
import jax.numpy as jnp
from jax import lax

NZ = 128
STEPS = 4
TF_BUMPS = 8
NX = 128
NY = 128
TFS = 8


lattice_velocities = ((0, 0, 0), (1, 0, 0), (-1, 0, 0), (0, 1, 0), (0, -1, 0), (0, 0, 1), (0, 0, -1), (1, 1, 0), (-1, -1, 0), (1, -1, 0), (-1, 1, 0), (1, 0, 1), (-1, 0, -1), (1, 0, -1), (-1, 0, 1), (0, 1, 1), (0, -1, -1), (0, 1, -1), (0, -1, 1))


lattice_weights = (1.0 / 3.0,) + (1.0 / 18.0,) * 6 + (1.0 / 36.0,) * 12


def draw_populations(key, part):
    flow_key = jax.random.fold_in(key, 11)
    noise_key = jax.random.fold_in(key, 23)
    flow = jnp.clip(0.05 * jax.random.normal(flow_key, (3, NX, NY, NZ), jnp.float32), -0.12, 0.12)
    noise = jax.random.uniform(noise_key, (19, NX, NY, NZ), jnp.float32, -0.1, 0.1)
    pieces = []
    for number in range(19):
        project = jnp.zeros((NX, NY, NZ), jnp.float32)
        for axis_index in range(3):
            factor = lattice_velocities[number][axis_index]
            if factor != 0:
                project = project + factor * flow[axis_index]
        pieces.append(lattice_weights[number] * (1.0 + 3.0 * project + noise[number]))
    return jnp.stack(pieces).astype(jnp.float32)


def place_ends(drawn, rng, least, top_value):
    longest = drawn.shape.index(max(drawn.shape))
    spots = []
    for shift in (0, 1):
        where = [jax.random.randint(jax.random.fold_in(rng, axis), (), 0, length) for axis, length in enumerate(drawn.shape)]
        where[longest] = (where[longest] + shift) % drawn.shape[longest]
        spots.append(tuple(where))
    return drawn.at[spots[0]].set(least).at[spots[1]].set(top_value)


def level_of(rng, shape, split, least, top_value):
    loudness, own = 1.0, jax.random.fold_in(rng, 6)
    for dim, parts in split:
        heights = jnp.exp(jax.random.uniform(jax.random.fold_in(own, dim), (parts,), jnp.float32, least / len(split), top_value / len(split)))
        loudness = loudness * jnp.repeat(heights, shape[dim] // parts).reshape([-1 if axis == dim else 1 for axis in range(len(shape))])
    return loudness


def setup_inputs(seed: int = 0) -> dict:
    splits = jax.random.split(jax.random.key(seed), 4)
    return {
        "populations": draw_populations(jax.random.fold_in(splits[3], 71), 0),
        "transfer": jnp.clip(0.1 + 0.9 * jax.random.uniform(splits[1], (TFS, 5, TF_BUMPS), jnp.float32) ** level_of(splits[1], (TFS, 5, TF_BUMPS), ((0, 8),), -0.2, 0.2), 0.1, 1.0),
        "direction": place_ends(jax.random.randint(splits[2], (TFS,), 0, 2), jax.random.fold_in(splits[2], 1), 0, 1).astype(jnp.int32),
    }


lattice_velocities = ((0, 0, 0), (1, 0, 0), (-1, 0, 0), (0, 1, 0), (0, -1, 0), (0, 0, 1), (0, 0, -1), (1, 1, 0), (-1, -1, 0), (1, -1, 0), (-1, 1, 0), (1, 0, 1), (-1, 0, -1), (1, 0, -1), (-1, 0, 1), (0, 1, 1), (0, -1, -1), (0, 1, -1), (0, -1, 1))
lattice_weights = (1.0 / 3.0,) + (1.0 / 18.0,) * 6 + (1.0 / 36.0,) * 12
relaxation = 1.25
bump_width = 0.15
level_offset = 0.05

def moments(field):
    density = field[0]
    for number in range(1, 19):
        density = density + field[number]
    components = []
    for axis_index in range(3):
        total = jnp.zeros_like(density)
        for number in range(19):
            factor = lattice_velocities[number][axis_index]
            if factor != 0:
                total = total + factor * field[number]
        components.append(total / density)
    return (density, components)

def collide(field):
    density, flow = moments(field)
    squared = flow[0] * flow[0] + flow[1] * flow[1] + flow[2] * flow[2]
    result = []
    for number in range(19):
        project = jnp.zeros_like(density)
        for axis_index in range(3):
            factor = lattice_velocities[number][axis_index]
            if factor != 0:
                project = project + factor * flow[axis_index]
        equilibrium = lattice_weights[number] * density * (1.0 + 3.0 * project + 4.5 * project * project - 1.5 * squared)
        result.append(field[number] - relaxation * (field[number] - equilibrium))
    return result

def slope(values, axis_index):
    return (jnp.roll(values, -1, axis_index) - jnp.roll(values, 1, axis_index)) * 0.5

def reference(populations, transfer, direction):
    field = populations
    for turn_index in range(STEPS):
        collided = collide(field)
        field = jnp.stack([jnp.roll(collided[number], lattice_velocities[number], axis=(0, 1, 2)) for number in range(19)])
    density, flow = moments(field)
    spin_x = slope(flow[2], 1) - slope(flow[1], 2)
    spin_y = slope(flow[0], 2) - slope(flow[2], 0)
    spin_z = slope(flow[1], 0) - slope(flow[0], 1)
    vorticity = jnp.sqrt(spin_x * spin_x + spin_y * spin_y + spin_z * spin_z).astype(jnp.bfloat16)
    level = vorticity.astype(jnp.float32)
    level = level / (level + level_offset)

    def render_one(pair):
        params, flip = pair
        extinction = jnp.zeros_like(level)
        emission = [jnp.zeros_like(level) for channel in range(3)]
        for bump_index in range(TF_BUMPS):
            bump = jnp.exp(-jnp.square((level - params[0, bump_index]) / bump_width))
            extinction = extinction + params[1, bump_index] * bump
            for channel in range(3):
                emission[channel] = emission[channel] + params[2 + channel, bump_index] * bump
        optical = extinction / NX
        inclusive = jnp.cumsum(optical, axis=0)
        total = inclusive[-1]
        front = jnp.where(flip == 1, total[None] - inclusive, inclusive - optical)
        weight = jnp.exp(-front) * (1.0 - jnp.exp(-optical))
        colors = [lax.optimization_barrier(jnp.sum(weight * emission[channel], axis=0)) for channel in range(3)]
        return jnp.stack(colors + [1.0 - jnp.exp(-total)])
    images = lax.map(render_one, (transfer, direction))
    return (field, vorticity, images)
```

```python
import functools
import math

import jax
import jax.numpy as jnp
from jax import lax
from jax.experimental import pallas as pl
from jax.experimental.pallas import tpu as pltpu
from jax.sharding import PartitionSpec as P

STEPS = 4
MESH = pl.DeviceIdType.MESH

lattice_velocities = (
    (0, 0, 0),
    (1, 0, 0),
    (-1, 0, 0),
    (0, 1, 0),
    (0, -1, 0),
    (0, 0, 1),
    (0, 0, -1),
    (1, 1, 0),
    (-1, -1, 0),
    (1, -1, 0),
    (-1, 1, 0),
    (1, 0, 1),
    (-1, 0, -1),
    (1, 0, -1),
    (-1, 0, 1),
    (0, 1, 1),
    (0, -1, -1),
    (0, 1, -1),
    (0, -1, 1),
)
relaxation = 1.25
bump_width = 0.15
level_offset = 0.05
LOG2E = math.log2(math.e)
SCALE = math.sqrt(LOG2E) / bump_width

COUNT = len(lattice_velocities)
ORDER = (
    [n for n in range(COUNT) if lattice_velocities[n][0] == 1]
    + [n for n in range(COUNT) if lattice_velocities[n][0] == -1]
    + [n for n in range(COUNT) if lattice_velocities[n][0] == 0]
)
SLOT = {number: place for place, number in enumerate(ORDER)}
UP_Y = [n for n in range(COUNT) if lattice_velocities[n][1] == 1]
DOWN_Y = [n for n in range(COUNT) if lattice_velocities[n][1] == -1]
CROSS = len(UP_Y)
CORNERS = [n for n in range(COUNT) if lattice_velocities[n][0] and lattice_velocities[n][1]]
PAIRS = [(n, n + 1) for n in range(1, COUNT, 2)]
LOW = 8
ROWS = 8


def add_all(values):
    while len(values) > 1:
        paired = [a + b for a, b in zip(values[0::2], values[1::2])]
        values = paired + ([values[-1]] if len(values) % 2 else [])
    return values[0]


def moments(field):
    diffs = {}
    sums = [field[0]]
    for plus, minus in PAIRS:
        sums.append(field[plus] + field[minus])
        diffs[plus] = field[plus] - field[minus]
    momentum = []
    for axis in range(3):
        total = diffs[1 + 2 * axis]
        for plus, _ in PAIRS[3:]:
            factor = lattice_velocities[plus][axis]
            if factor == 1:
                total = total + diffs[plus]
            elif factor == -1:
                total = total - diffs[plus]
        momentum.append(total)
    return add_all(sums), momentum


def collide(field):
    density, momentum = moments(field)
    inverse = 1.0 / density
    square = momentum[0] * momentum[0] + momentum[1] * momentum[1] + momentum[2] * momentum[2]
    even = density - 1.5 * (square * inverse)
    keep = 1.0 - relaxation
    result = [keep * field[0] + (relaxation / 3.0) * even] + [None] * (COUNT - 1)
    parts = {}
    for divisor in (18.0, 36.0):
        parts[divisor] = ((relaxation / divisor) * even, (relaxation * 4.5 / divisor) * inverse)
    for plus, minus in PAIRS:
        project = None
        for axis in range(3):
            factor = lattice_velocities[plus][axis]
            if factor:
                if project is None:
                    project = momentum[axis]
                elif factor == 1:
                    project = project + momentum[axis]
                else:
                    project = project - momentum[axis]
        divisor = 18.0 if plus < 7 else 36.0
        base, curve = parts[divisor]
        symmetric = base + curve * (project * project)
        odd = (3.0 * relaxation / divisor) * project
        result[plus] = keep * field[plus] + (symmetric + odd)
        result[minus] = keep * field[minus] + (symmetric - odd)
    return result


def kernel(
    sizes,
    f_hbm,
    par,
    direct,
    fout,
    vort,
    img,
    F,
    A,
    B,
    SY,
    RY,
    SC,
    RC,
    U,
    VS,
    VR,
    L,
    PA,
    PS,
    PR,
    in_sem,
    out_sem,
    halo_s,
    halo_r,
    flow_s,
    flow_r,
    pa_s,
    pa_r,
    pr_s,
    pr_r,
):
    nd, ni, X, W, NZ, bumps = sizes
    d = lax.axis_index("depth")
    i = lax.axis_index("image")
    halves = W // ROWS
    ratio = ni // nd
    chunks = 4
    step_x = X // chunks

    loads = [
        pltpu.make_async_copy(
            f_hbm.at[:, pl.ds(c * step_x, step_x)],
            F.at[:, pl.ds(c * step_x, step_x)],
            in_sem.at[c],
        )
        for c in range(chunks)
    ]
    for copy in loads:
        copy.start()

    barrier = pltpu.get_barrier_semaphore()
    everyone = nd * ni
    me = d * ni + i

    def greet(offset, carry):
        other = lax.rem(me + offset, everyone)
        pl.semaphore_signal(
            barrier,
            inc=1,
            device_id={"depth": other // ni, "image": lax.rem(other, ni)},
            device_id_type=MESH,
        )
        return carry

    lax.fori_loop(1, everyone, greet, 0)

    ray = X * nd
    for k in range(bumps):
        for kind in range(5):
            factor = SCALE if kind == 0 else (LOG2E / ray if kind == 1 else 1.0)
            value = par[0, kind, k] * factor
            PA[i, pl.ds(kind * bumps + k, 1), :] = jnp.full((1, NZ), value, jnp.float32)
    PA[i, pl.ds(5 * bumps, 1), :] = jnp.full((1, NZ), direct[0].astype(jnp.float32), jnp.float32)

    def to(cx, cy):
        return {"depth": lax.rem(d + cx + nd, nd), "image": lax.rem(i + cy + ni, ni)}

    def remote(src, dst, send, recv, target):
        return pltpu.make_async_remote_copy(
            src_ref=src,
            dst_ref=dst,
            send_sem=send,
            recv_sem=recv,
            device_id=target,
            device_id_type=MESH,
        )

    def store(D, x, h, values):
        for number in range(COUNT):
            D[SLOT[number], x + 1, pl.ds(LOW + ROWS * h, ROWS), :] = values[number]
        if h == 0:
            for j, number in enumerate(DOWN_Y):
                SY[0, j, pl.ds(x, 1), :] = values[number][0:1]
        if h == halves - 1:
            for j, number in enumerate(UP_Y):
                SY[1, j, pl.ds(x, 1), :] = values[number][ROWS - 1 : ROWS]

    def streamed(S, x, h):
        field = []
        for number in range(COUNT):
            cx, cy, cz = lattice_velocities[number]
            value = S[SLOT[number], x + 1 - cx, pl.ds(LOW + ROWS * h - cy, ROWS), :]
            if cz:
                value = pltpu.roll(value, cz % NZ, 1)
            field.append(value)
        return field

    def exchange(D, turn):
        slot = turn % 2
        for k, number in enumerate(CORNERS):
            cx, cy, _ = lattice_velocities[number]
            group = UP_Y if cy == 1 else DOWN_Y
            edge = X - 1 if cx == 1 else 0
            SC[k, 0:1, :] = SY[1 if cy == 1 else 0, group.index(number), edge : edge + 1, :]
        inner = pl.ds(LOW, W)
        copies = []

        def add(src, dst, target):
            k = len(copies)
            copies.append(remote(src, dst, halo_s.at[turn, k], halo_r.at[turn, k], target))

        add(SY.at[1], RY.at[slot, 1], to(0, 1))
        add(SY.at[0], RY.at[slot, 0], to(0, -1))
        for k, number in enumerate(CORNERS):
            cx, cy, _ = lattice_velocities[number]
            add(SC.at[k], RC.at[slot, k], to(cx, cy))
        add(D.at[pl.ds(0, CROSS), X, inner], D.at[pl.ds(0, CROSS), 0, inner], to(1, 0))
        add(D.at[pl.ds(CROSS, CROSS), 1, inner], D.at[pl.ds(CROSS, CROSS), X + 1, inner], to(-1, 0))
        for copy in copies:
            copy.start()
        for copy in copies:
            copy.wait()

        def unpack(x, carry):
            for j, number in enumerate(UP_Y):
                D[SLOT[number], x + 1, pl.ds(LOW - 1, 1), :] = RY[slot, 1, j, pl.ds(x, 1), :]
            for j, number in enumerate(DOWN_Y):
                D[SLOT[number], x + 1, pl.ds(LOW + W, 1), :] = RY[slot, 0, j, pl.ds(x, 1), :]
            return carry

        lax.fori_loop(0, X, unpack, 0)
        for k, number in enumerate(CORNERS):
            cx, cy, _ = lattice_velocities[number]
            row = LOW - 1 if cy == 1 else LOW + W
            D[SLOT[number], 0 if cx == 1 else X + 1, row : row + 1, :] = RC[slot, k, 0:1, :]

    def first(x, carry):
        for h in range(halves):
            field = [F[number, x, pl.ds(ROWS * h, ROWS), :] for number in range(COUNT)]
            store(A, x, h, collide(field))
        return carry

    for c in range(chunks):
        loads[c].wait()
        lax.fori_loop(c * step_x, (c + 1) * step_x, first, 0)

    pl.semaphore_wait(barrier, everyone - 1)
    shares = [
        remote(PA.at[i], PA.at[i], pa_s.at[o], pa_r.at[o], to(0, o)) for o in range(1, ni)
    ]
    exchange(A, 0)
    for copy in shares:
        copy.start()

    source, target = A, B
    for turn in range(1, STEPS):

        def middle(x, carry, source=source, target=target):
            for h in range(halves):
                store(target, x, h, collide(streamed(source, x, h)))
            return carry

        lax.fori_loop(0, X, middle, 0)
        exchange(target, turn)
        source, target = target, source

    def last(x, carry):
        for h in range(halves):
            field = streamed(source, x, h)
            for number in range(COUNT):
                F[number, x, pl.ds(ROWS * h, ROWS), :] = field[number]
            density, momentum = moments(field)
            inverse = 1.0 / density
            flow = [part * inverse for part in momentum]
            for place, axis in enumerate((1, 2, 0)):
                U[place, x + 1, pl.ds(LOW + ROWS * h, ROWS), :] = flow[axis]
            if h == 0:
                VS[0, 0, pl.ds(x, 1), :] = flow[2][0:1]
                VS[0, 1, pl.ds(x, 1), :] = flow[0][0:1]
            if h == halves - 1:
                VS[1, 0, pl.ds(x, 1), :] = flow[2][ROWS - 1 : ROWS]
                VS[1, 1, pl.ds(x, 1), :] = flow[0][ROWS - 1 : ROWS]
        return carry

    lax.fori_loop(0, X, last, 0)
    inner = pl.ds(LOW, W)
    flows = [
        remote(VS.at[1], VR.at[1], flow_s.at[0], flow_r.at[0], to(0, 1)),
        remote(VS.at[0], VR.at[0], flow_s.at[1], flow_r.at[1], to(0, -1)),
        remote(
            U.at[pl.ds(0, 2), X, inner],
            U.at[pl.ds(0, 2), 0, inner],
            flow_s.at[2],
            flow_r.at[2],
            to(1, 0),
        ),
        remote(
            U.at[pl.ds(0, 2), 1, inner],
            U.at[pl.ds(0, 2), X + 1, inner],
            flow_s.at[3],
            flow_r.at[3],
            to(-1, 0),
        ),
    ]
    for copy in flows:
        copy.start()
    out = pltpu.make_async_copy(F, fout, out_sem)
    out.start()
    for copy in shares:
        copy.wait()
    for copy in flows:
        copy.wait()

    def flow_rows(x, carry):
        for place, j in ((1, 0), (2, 1)):
            U[place, x + 1, pl.ds(LOW - 1, 1), :] = VR[1, j, pl.ds(x, 1), :]
            U[place, x + 1, pl.ds(LOW + W, 1), :] = VR[0, j, pl.ds(x, 1), :]
        return carry

    lax.fori_loop(0, X, flow_rows, 0)

    def spin(x, carry):
        def across_x(place):
            return (U[place, x + 2, inner, :] - U[place, x, inner, :]) * 0.5

        def across_y(place):
            above = U[place, x + 1, pl.ds(LOW + 1, W), :]
            return (above - U[place, x + 1, pl.ds(LOW - 1, W), :]) * 0.5

        def across_z(place):
            value = U[place, x + 1, inner, :]
            return (pltpu.roll(value, NZ - 1, 1) - pltpu.roll(value, 1, 1)) * 0.5

        spin_x = across_y(1) - across_z(0)
        spin_y = across_z(2) - across_x(1)
        spin_z = across_x(0) - across_y(2)
        size = jnp.sqrt(spin_x * spin_x + spin_y * spin_y + spin_z * spin_z)
        rounded = size.astype(jnp.bfloat16)
        vort[x] = rounded
        value = rounded.astype(jnp.float32)
        L[x] = (value / (value + level_offset)) * SCALE
        return carry

    lax.fori_loop(0, X, spin, 0)

    owner = i // ratio
    mine = d * ratio + lax.rem(i, ratio)

    def row(m, r):
        return jnp.broadcast_to(PA[m, pl.ds(r, 1), :], (ROWS, NZ))

    def blend(backward, through, colors, local_through, local_colors):
        fade = jnp.where(backward, local_through, 1.0)
        lit = jnp.where(backward, 1.0, through)
        mixed = [color * fade + lit * local for color, local in zip(colors, local_colors)]
        return through * local_through, mixed

    def piece(o, m):
        return remote(
            PS.at[m],
            PR.at[mine],
            pr_s.at[o],
            pr_r.at[mine],
            {"depth": owner, "image": m},
        )

    def render(o, carry):
        m = lax.rem(i + 1 + o, ni)
        backward = row(m, 5 * bumps) > 0.5

        def along(x, state):
            new = []
            levels = [L[x, pl.ds(ROWS * h, ROWS), :] for h in range(halves)]
            totals = [[None] * 4 for h in range(halves)]
            for k in range(bumps):
                centre = row(m, k)
                gains = [row(m, (1 + j) * bumps + k) for j in range(4)]
                for h in range(halves):
                    offset = levels[h] - centre
                    bump = jnp.exp2(-(offset * offset))
                    for j in range(4):
                        term = gains[j] * bump
                        totals[h][j] = term if k == 0 else totals[h][j] + term
            for h in range(halves):
                through, colors = state[4 * h], state[4 * h + 1 : 4 * h + 4]
                local = jnp.exp2(-totals[h][0])
                alpha = 1.0 - local
                shades = [alpha * total for total in totals[h][1:]]
                through, colors = blend(backward, through, colors, local, shades)
                new += [through] + list(colors)
            return tuple(new)

        zero = jnp.zeros((ROWS, NZ), jnp.float32)
        start = (jnp.ones((ROWS, NZ), jnp.float32), zero, zero, zero) * halves
        state = lax.fori_loop(0, X, along, start)
        for h in range(halves):
            through, colors = state[4 * h], state[4 * h + 1 : 4 * h + 4]
            for j, value in enumerate(list(colors) + [through]):
                PS[m, j, pl.ds(ROWS * h, ROWS), :] = value
        local_target = jnp.logical_and(owner == d, m == i)

        @pl.when(local_target)
        def _():
            PR[mine] = PS[m]

        @pl.when(jnp.logical_not(local_target))
        def _():
            piece(o, m).start()

        return carry

    lax.fori_loop(0, ni, render, 0)

    def sent(o, carry):
        m = lax.rem(i + 1 + o, ni)

        @pl.when(jnp.logical_not(jnp.logical_and(owner == d, m == i)))
        def _():
            piece(o, m).wait_send()

        return carry

    def arrived(slot, carry):
        @pl.when(jnp.logical_not(jnp.logical_and(owner == d, slot == mine)))
        def _():
            remote(
                PS.at[0], PR.at[slot], pr_s.at[0], pr_r.at[slot], {"depth": d, "image": i}
            ).wait_recv()

        return carry

    lax.fori_loop(0, nd * ratio, arrived, 0)
    backward = row(i, 5 * bumps) > 0.5
    for part in range(ratio):
        for h in range(halves):
            rows = pl.ds(ROWS * h, ROWS)
            through = jnp.ones((ROWS, NZ), jnp.float32)
            colors = [jnp.zeros((ROWS, NZ), jnp.float32)] * 3
            for slab in range(nd):
                slot = slab * ratio + part
                local = [PR[slot, j, rows, :] for j in range(4)]
                through, colors = blend(backward, through, colors, local[3], local[:3])
            for j, value in enumerate(colors + [1.0 - through]):
                img[0, j, pl.ds(part * W + ROWS * h, ROWS), :] = value
    lax.fori_loop(0, ni, sent, 0)
    out.wait()


def on_device(populations, transfer, direction):
    nd, ni = lax.axis_size("depth"), lax.axis_size("image")
    count, X, W, NZ = populations.shape
    bumps = transfer.shape[2]
    assert transfer.shape[0] == 1 and ni % nd == 0 and W % ROWS == 0 and X % 8 == 0
    sizes = (nd, ni, X, W, NZ, bumps)
    ratio = ni // nd
    padded = W + 2 * ROWS
    f32 = jnp.float32
    table = -(-(5 * bumps + 1) // 8) * 8
    dma = pltpu.SemaphoreType.DMA
    return pl.pallas_call(
        functools.partial(kernel, sizes),
        out_shape=(
            jax.ShapeDtypeStruct(populations.shape, f32),
            jax.ShapeDtypeStruct((X, W, NZ), jnp.bfloat16),
            jax.ShapeDtypeStruct((1, 4, ratio * W, NZ), f32),
        ),
        in_specs=[
            pl.BlockSpec(memory_space=pl.ANY),
            pl.BlockSpec(memory_space=pltpu.SMEM),
            pl.BlockSpec(memory_space=pltpu.SMEM),
        ],
        out_specs=(
            pl.BlockSpec(memory_space=pl.ANY),
            pl.BlockSpec(memory_space=pltpu.VMEM),
            pl.BlockSpec(memory_space=pltpu.VMEM),
        ),
        scratch_shapes=[
            pltpu.VMEM((COUNT, X, W, NZ), f32),
            pltpu.VMEM((COUNT, X + 2, padded, NZ), f32),
            pltpu.VMEM((COUNT, X + 2, padded, NZ), f32),
            pltpu.VMEM((2, CROSS, X, NZ), f32),
            pltpu.VMEM((2, 2, CROSS, X, NZ), f32),
            pltpu.VMEM((4, 8, NZ), f32),
            pltpu.VMEM((2, 4, 8, NZ), f32),
            pltpu.VMEM((3, X + 2, padded, NZ), f32),
            pltpu.VMEM((2, 2, X, NZ), f32),
            pltpu.VMEM((2, 2, X, NZ), f32),
            pltpu.VMEM((X, W, NZ), f32),
            pltpu.VMEM((ni, table, NZ), f32),
            pltpu.VMEM((ni, 4, W, NZ), f32),
            pltpu.VMEM((nd * ratio, 4, W, NZ), f32),
            dma((4,)),
            dma(()),
            dma((STEPS, 8)),
            dma((STEPS, 8)),
            dma((4,)),
            dma((4,)),
            dma((ni,)),
            dma((ni,)),
            dma((ni,)),
            dma((nd * ratio,)),
        ],
        compiler_params=pltpu.CompilerParams(
            collective_id=0, has_side_effects=True, vmem_limit_bytes=56 << 20
        ),
    )(populations, transfer, direction)


def solution(mesh):
    in_specs = (P(None, "depth", "image", None), P("image", None, None), P("image"))
    out_specs = (
        P(None, "depth", "image", None),
        P("depth", "image", None),
        P("image", None, "depth", None),
    )
    return jax.shard_map(
        on_device, mesh=mesh, in_specs=in_specs, out_specs=out_specs, check_vma=False
    )
```

```python
import functools
import math

import jax
import jax.numpy as jnp
from jax import lax
from jax.experimental import pallas as pl
from jax.experimental.pallas import tpu as pltpu
from jax.sharding import PartitionSpec as P

STEPS = 4
MESH = pl.DeviceIdType.MESH

lattice_velocities = (
    (0, 0, 0),
    (1, 0, 0),
    (-1, 0, 0),
    (0, 1, 0),
    (0, -1, 0),
    (0, 0, 1),
    (0, 0, -1),
    (1, 1, 0),
    (-1, -1, 0),
    (1, -1, 0),
    (-1, 1, 0),
    (1, 0, 1),
    (-1, 0, -1),
    (1, 0, -1),
    (-1, 0, 1),
    (0, 1, 1),
    (0, -1, -1),
    (0, 1, -1),
    (0, -1, 1),
)
relaxation = 1.25
bump_width = 0.15
level_offset = 0.05
LOG2E = math.log2(math.e)
SCALE = math.sqrt(LOG2E) / bump_width

COUNT = len(lattice_velocities)
ORDER = (
    [n for n in range(COUNT) if lattice_velocities[n][0] == 1]
    + [n for n in range(COUNT) if lattice_velocities[n][0] == -1]
    + [n for n in range(COUNT) if lattice_velocities[n][0] == 0]
)
SLOT = {number: place for place, number in enumerate(ORDER)}
UP_Y = [n for n in range(COUNT) if lattice_velocities[n][1] == 1]
DOWN_Y = [n for n in range(COUNT) if lattice_velocities[n][1] == -1]
CROSS = len(UP_Y)
CORNERS = [n for n in range(COUNT) if lattice_velocities[n][0] and lattice_velocities[n][1]]
PAIRS = [(n, n + 1) for n in range(1, COUNT, 2)]
LOW = 8
ROWS = 8


def add_all(values):
    while len(values) > 1:
        paired = [a + b for a, b in zip(values[0::2], values[1::2])]
        values = paired + ([values[-1]] if len(values) % 2 else [])
    return values[0]


def moments(field):
    diffs = {}
    sums = [field[0]]
    for plus, minus in PAIRS:
        sums.append(field[plus] + field[minus])
        diffs[plus] = field[plus] - field[minus]
    momentum = []
    for axis in range(3):
        total = diffs[1 + 2 * axis]
        for plus, _ in PAIRS[3:]:
            factor = lattice_velocities[plus][axis]
            if factor == 1:
                total = total + diffs[plus]
            elif factor == -1:
                total = total - diffs[plus]
        momentum.append(total)
    return add_all(sums), momentum


def collide(field):
    density, momentum = moments(field)
    inverse = 1.0 / density
    square = momentum[0] * momentum[0] + momentum[1] * momentum[1] + momentum[2] * momentum[2]
    even = density - 1.5 * (square * inverse)
    keep = 1.0 - relaxation
    result = [keep * field[0] + (relaxation / 3.0) * even] + [None] * (COUNT - 1)
    parts = {}
    for divisor in (18.0, 36.0):
        parts[divisor] = ((relaxation / divisor) * even, (relaxation * 4.5 / divisor) * inverse)
    for plus, minus in PAIRS:
        project = None
        for axis in range(3):
            factor = lattice_velocities[plus][axis]
            if factor:
                if project is None:
                    project = momentum[axis]
                elif factor == 1:
                    project = project + momentum[axis]
                else:
                    project = project - momentum[axis]
        divisor = 18.0 if plus < 7 else 36.0
        base, curve = parts[divisor]
        symmetric = base + curve * (project * project)
        odd = (3.0 * relaxation / divisor) * project
        result[plus] = keep * field[plus] + (symmetric + odd)
        result[minus] = keep * field[minus] + (symmetric - odd)
    return result


def kernel(
    sizes,
    f_hbm,
    par,
    direct,
    F,
    vort,
    img,
    A,
    B,
    SY,
    RY,
    SC,
    RC,
    U,
    VS,
    VR,
    L,
    PC,
    PA,
    PS,
    PR,
    in_sem,
    halo_s,
    halo_r,
    flow_s,
    flow_r,
    pa_s,
    pa_r,
    pr_s,
    pr_r,
):
    nd, ni, X, W, NZ, bumps = sizes
    d = lax.axis_index("depth")
    i = lax.axis_index("image")
    halves = W // ROWS
    ratio = ni // nd
    chunks = 4
    step_x = X // chunks

    loads = [
        pltpu.make_async_copy(
            f_hbm.at[:, pl.ds(c * step_x, step_x)],
            F.at[:, pl.ds(c * step_x, step_x)],
            in_sem.at[c],
        )
        for c in range(chunks)
    ]
    for copy in loads:
        copy.start()

    barrier = pltpu.get_barrier_semaphore()
    everyone = nd * ni
    me = d * ni + i

    def greet(offset, carry):
        other = lax.rem(me + offset, everyone)
        pl.semaphore_signal(
            barrier,
            inc=1,
            device_id={"depth": other // ni, "image": lax.rem(other, ni)},
            device_id_type=MESH,
        )
        return carry

    lax.fori_loop(1, everyone, greet, 0)

    ray = X * nd
    lane = lax.broadcasted_iota(jnp.int32, (8, NZ), 1)
    entries = jnp.full((8, NZ), direct[0].astype(jnp.float32), jnp.float32)
    for k in range(bumps):
        for kind in range(5):
            factor = SCALE if kind == 0 else (LOG2E / ray if kind == 1 else 1.0)
            entries = jnp.where(lane == kind * bumps + k, par[kind, 0, k] * factor, entries)
    PC[i] = entries

    def to(cx, cy):
        return {"depth": lax.rem(d + cx + nd, nd), "image": lax.rem(i + cy + ni, ni)}

    def remote(src, dst, send, recv, target):
        return pltpu.make_async_remote_copy(
            src_ref=src,
            dst_ref=dst,
            send_sem=send,
            recv_sem=recv,
            device_id=target,
            device_id_type=MESH,
        )

    def store(D, x, h, values):
        for number in range(COUNT):
            D[SLOT[number], x + 1, pl.ds(LOW + ROWS * h, ROWS), :] = values[number]
        if h == 0:
            for j, number in enumerate(DOWN_Y):
                SY[0, j, pl.ds(x, 1), :] = values[number][0:1]
        if h == halves - 1:
            for j, number in enumerate(UP_Y):
                SY[1, j, pl.ds(x, 1), :] = values[number][ROWS - 1 : ROWS]

    def streamed(S, x, h):
        field = []
        for number in range(COUNT):
            cx, cy, cz = lattice_velocities[number]
            value = S[SLOT[number], x + 1 - cx, pl.ds(LOW + ROWS * h - cy, ROWS), :]
            if cz:
                value = pltpu.roll(value, cz % NZ, 1)
            field.append(value)
        return field

    def exchange(D, turn):
        slot = turn % 2
        for k, number in enumerate(CORNERS):
            cx, cy, _ = lattice_velocities[number]
            group = UP_Y if cy == 1 else DOWN_Y
            edge = X - 1 if cx == 1 else 0
            SC[k, 0:1, :] = SY[1 if cy == 1 else 0, group.index(number), edge : edge + 1, :]
        inner = pl.ds(LOW, W)
        copies = []

        def add(src, dst, target):
            k = len(copies)
            copies.append(remote(src, dst, halo_s.at[turn, k], halo_r.at[turn, k], target))

        add(SY.at[1], RY.at[slot, 1], to(0, 1))
        add(SY.at[0], RY.at[slot, 0], to(0, -1))
        for k, number in enumerate(CORNERS):
            cx, cy, _ = lattice_velocities[number]
            add(SC.at[k], RC.at[slot, k], to(cx, cy))
        add(D.at[pl.ds(0, CROSS), X, inner], D.at[pl.ds(0, CROSS), 0, inner], to(1, 0))
        add(D.at[pl.ds(CROSS, CROSS), 1, inner], D.at[pl.ds(CROSS, CROSS), X + 1, inner], to(-1, 0))
        for copy in copies:
            copy.start()
        for copy in copies:
            copy.wait()

        def unpack(x, carry):
            for j, number in enumerate(UP_Y):
                D[SLOT[number], x + 1, pl.ds(LOW - 1, 1), :] = RY[slot, 1, j, pl.ds(x, 1), :]
            for j, number in enumerate(DOWN_Y):
                D[SLOT[number], x + 1, pl.ds(LOW + W, 1), :] = RY[slot, 0, j, pl.ds(x, 1), :]
            return carry

        lax.fori_loop(0, X, unpack, 0)
        for k, number in enumerate(CORNERS):
            cx, cy, _ = lattice_velocities[number]
            row = LOW - 1 if cy == 1 else LOW + W
            D[SLOT[number], 0 if cx == 1 else X + 1, row : row + 1, :] = RC[slot, k, 0:1, :]

    def first(x, carry):
        for h in range(halves):
            field = [F[number, x, pl.ds(ROWS * h, ROWS), :] for number in range(COUNT)]
            store(A, x, h, collide(field))
        return carry

    for c in range(chunks):
        loads[c].wait()
        lax.fori_loop(c * step_x, (c + 1) * step_x, first, 0)

    pl.semaphore_wait(barrier, everyone - 1)
    shares = [
        remote(PC.at[i], PC.at[i], pa_s.at[o], pa_r.at[o], to(0, o)) for o in range(1, ni)
    ]
    exchange(A, 0)
    for copy in shares:
        copy.start()

    source, target = A, B
    for turn in range(1, STEPS):

        def middle(x, carry, source=source, target=target):
            for h in range(halves):
                store(target, x, h, collide(streamed(source, x, h)))
            return carry

        lax.fori_loop(0, X, middle, 0)
        exchange(target, turn)
        source, target = target, source

    def last(x, carry):
        for h in range(halves):
            field = streamed(source, x, h)
            for number in range(COUNT):
                F[number, x, pl.ds(ROWS * h, ROWS), :] = field[number]
            density, momentum = moments(field)
            inverse = 1.0 / density
            flow = [part * inverse for part in momentum]
            for place, axis in enumerate((1, 2, 0)):
                U[place, x + 1, pl.ds(LOW + ROWS * h, ROWS), :] = flow[axis]
            if h == 0:
                VS[0, 0, pl.ds(x, 1), :] = flow[2][0:1]
                VS[0, 1, pl.ds(x, 1), :] = flow[0][0:1]
            if h == halves - 1:
                VS[1, 0, pl.ds(x, 1), :] = flow[2][ROWS - 1 : ROWS]
                VS[1, 1, pl.ds(x, 1), :] = flow[0][ROWS - 1 : ROWS]
        return carry

    lax.fori_loop(0, X, last, 0)
    inner = pl.ds(LOW, W)
    flows = [
        remote(VS.at[1], VR.at[1], flow_s.at[0], flow_r.at[0], to(0, 1)),
        remote(VS.at[0], VR.at[0], flow_s.at[1], flow_r.at[1], to(0, -1)),
        remote(
            U.at[pl.ds(0, 2), X, inner],
            U.at[pl.ds(0, 2), 0, inner],
            flow_s.at[2],
            flow_r.at[2],
            to(1, 0),
        ),
        remote(
            U.at[pl.ds(0, 2), 1, inner],
            U.at[pl.ds(0, 2), X + 1, inner],
            flow_s.at[3],
            flow_r.at[3],
            to(-1, 0),
        ),
    ]
    for copy in flows:
        copy.start()
    for copy in shares:
        copy.wait()

    def expand(m, carry):
        for block in range(PA.shape[1] // 8):
            line = lax.broadcasted_iota(jnp.int32, (8, NZ), 0) + 8 * block
            chosen = jnp.where(lane == line, PC[m], 0.0)
            value = jnp.sum(chosen, axis=1, keepdims=True)
            PA[m, pl.ds(8 * block, 8), :] = jnp.broadcast_to(value, (8, NZ))
        return carry

    lax.fori_loop(0, ni, expand, 0)
    for copy in flows:
        copy.wait()

    def flow_rows(x, carry):
        for place, j in ((1, 0), (2, 1)):
            U[place, x + 1, pl.ds(LOW - 1, 1), :] = VR[1, j, pl.ds(x, 1), :]
            U[place, x + 1, pl.ds(LOW + W, 1), :] = VR[0, j, pl.ds(x, 1), :]
        return carry

    lax.fori_loop(0, X, flow_rows, 0)

    def spin(x, carry):
        def across_x(place):
            return (U[place, x + 2, inner, :] - U[place, x, inner, :]) * 0.5

        def across_y(place):
            above = U[place, x + 1, pl.ds(LOW + 1, W), :]
            return (above - U[place, x + 1, pl.ds(LOW - 1, W), :]) * 0.5

        def across_z(place):
            value = U[place, x + 1, inner, :]
            return (pltpu.roll(value, NZ - 1, 1) - pltpu.roll(value, 1, 1)) * 0.5

        spin_x = across_y(1) - across_z(0)
        spin_y = across_z(2) - across_x(1)
        spin_z = across_x(0) - across_y(2)
        size = jnp.sqrt(spin_x * spin_x + spin_y * spin_y + spin_z * spin_z)
        rounded = size.astype(jnp.bfloat16)
        vort[x] = rounded
        value = rounded.astype(jnp.float32)
        L[x] = (value / (value + level_offset)) * SCALE
        return carry

    lax.fori_loop(0, X, spin, 0)

    owner = i // ratio
    mine = d * ratio + lax.rem(i, ratio)

    def row(m, r):
        return jnp.broadcast_to(PA[m, pl.ds(r, 1), :], (ROWS, NZ))

    def blend(backward, through, colors, local_through, local_colors):
        fade = jnp.where(backward, local_through, 1.0)
        lit = jnp.where(backward, 1.0, through)
        mixed = [color * fade + lit * local for color, local in zip(colors, local_colors)]
        return through * local_through, mixed

    def piece(o, m):
        return remote(
            PS.at[m],
            PR.at[mine],
            pr_s.at[o],
            pr_r.at[mine],
            {"depth": owner, "image": m},
        )

    def render(o, carry):
        m = lax.rem(i + 1 + o, ni)
        backward = row(m, 5 * bumps) > 0.5

        def along(x, state):
            new = []
            levels = [L[x, pl.ds(ROWS * h, ROWS), :] for h in range(halves)]
            totals = [[None] * 4 for h in range(halves)]
            for k in range(bumps):
                centre = row(m, k)
                gains = [row(m, (1 + j) * bumps + k) for j in range(4)]
                for h in range(halves):
                    offset = levels[h] - centre
                    bump = jnp.exp2(-(offset * offset))
                    for j in range(4):
                        term = gains[j] * bump
                        totals[h][j] = term if k == 0 else totals[h][j] + term
            for h in range(halves):
                through, colors = state[4 * h], state[4 * h + 1 : 4 * h + 4]
                local = jnp.exp2(-totals[h][0])
                alpha = 1.0 - local
                shades = [alpha * total for total in totals[h][1:]]
                through, colors = blend(backward, through, colors, local, shades)
                new += [through] + list(colors)
            return tuple(new)

        zero = jnp.zeros((ROWS, NZ), jnp.float32)
        start = (jnp.ones((ROWS, NZ), jnp.float32), zero, zero, zero) * halves
        state = lax.fori_loop(0, X, along, start)
        for h in range(halves):
            through, colors = state[4 * h], state[4 * h + 1 : 4 * h + 4]
            for j, value in enumerate(list(colors) + [through]):
                PS[m, j, pl.ds(ROWS * h, ROWS), :] = value
        local_target = jnp.logical_and(owner == d, m == i)

        @pl.when(local_target)
        def _():
            PR[mine] = PS[m]

        @pl.when(jnp.logical_not(local_target))
        def _():
            piece(o, m).start()

        return carry

    lax.fori_loop(0, ni, render, 0)

    def sent(o, carry):
        m = lax.rem(i + 1 + o, ni)

        @pl.when(jnp.logical_not(jnp.logical_and(owner == d, m == i)))
        def _():
            piece(o, m).wait_send()

        return carry

    def arrived(slot, carry):
        @pl.when(jnp.logical_not(jnp.logical_and(owner == d, slot == mine)))
        def _():
            remote(
                PS.at[0], PR.at[slot], pr_s.at[0], pr_r.at[slot], {"depth": d, "image": i}
            ).wait_recv()

        return carry

    lax.fori_loop(0, nd * ratio, arrived, 0)
    backward = row(i, 5 * bumps) > 0.5
    for part in range(ratio):
        for h in range(halves):
            rows = pl.ds(ROWS * h, ROWS)
            through = jnp.ones((ROWS, NZ), jnp.float32)
            colors = [jnp.zeros((ROWS, NZ), jnp.float32)] * 3
            for slab in range(nd):
                slot = slab * ratio + part
                local = [PR[slot, j, rows, :] for j in range(4)]
                through, colors = blend(backward, through, colors, local[3], local[:3])
            for j, value in enumerate(colors + [1.0 - through]):
                img[0, j, pl.ds(part * W + ROWS * h, ROWS), :] = value
    lax.fori_loop(0, ni, sent, 0)


def on_device(populations, transfer, direction):
    nd, ni = lax.axis_size("depth"), lax.axis_size("image")
    count, X, W, NZ = populations.shape
    bumps = transfer.shape[2]
    assert transfer.shape[0] == 1 and ni % nd == 0 and W % ROWS == 0 and X % 8 == 0
    sizes = (nd, ni, X, W, NZ, bumps)
    ratio = ni // nd
    padded = W + 2 * ROWS
    f32 = jnp.float32
    table = -(-(5 * bumps + 1) // 8) * 8
    dma = pltpu.SemaphoreType.DMA
    return pl.pallas_call(
        functools.partial(kernel, sizes),
        out_shape=(
            pltpu.VMEM(populations.shape, f32),
            jax.ShapeDtypeStruct((X, W, NZ), jnp.bfloat16),
            jax.ShapeDtypeStruct((1, 4, ratio * W, NZ), f32),
        ),
        in_specs=[
            pl.BlockSpec(memory_space=pl.ANY),
            pl.BlockSpec(memory_space=pltpu.SMEM),
            pl.BlockSpec(memory_space=pltpu.SMEM),
        ],
        out_specs=(
            pl.BlockSpec(memory_space=pltpu.VMEM),
            pl.BlockSpec(memory_space=pltpu.VMEM),
            pl.BlockSpec(memory_space=pltpu.VMEM),
        ),
        scratch_shapes=[
            pltpu.VMEM((COUNT, X + 2, padded, NZ), f32),
            pltpu.VMEM((COUNT, X + 2, padded, NZ), f32),
            pltpu.VMEM((2, CROSS, X, NZ), f32),
            pltpu.VMEM((2, 2, CROSS, X, NZ), f32),
            pltpu.VMEM((4, 8, NZ), f32),
            pltpu.VMEM((2, 4, 8, NZ), f32),
            pltpu.VMEM((3, X + 2, padded, NZ), f32),
            pltpu.VMEM((2, 2, X, NZ), f32),
            pltpu.VMEM((2, 2, X, NZ), f32),
            pltpu.VMEM((X, W, NZ), f32),
            pltpu.VMEM((ni, 8, NZ), f32),
            pltpu.VMEM((ni, table, NZ), f32),
            pltpu.VMEM((ni, 4, W, NZ), f32),
            pltpu.VMEM((nd * ratio, 4, W, NZ), f32),
            dma((4,)),
            dma((STEPS, 8)),
            dma((STEPS, 8)),
            dma((4,)),
            dma((4,)),
            dma((ni,)),
            dma((ni,)),
            dma((ni,)),
            dma((nd * ratio,)),
        ],
        compiler_params=pltpu.CompilerParams(
            collective_id=0, has_side_effects=True, vmem_limit_bytes=56 << 20
        ),
    )(populations, transfer.transpose(1, 0, 2), direction)


def solution(mesh):
    in_specs = (P(None, "depth", "image", None), P("image", None, None), P("image"))
    out_specs = (
        P(None, "depth", "image", None),
        P("depth", "image", None),
        P("image", None, "depth", None),
    )
    return jax.shard_map(
        on_device, mesh=mesh, in_specs=in_specs, out_specs=out_specs, check_vma=False
    )
```

```python
import functools
import math

import jax
import jax.numpy as jnp
from jax import lax
from jax.experimental import pallas as pl
from jax.experimental.pallas import tpu as pltpu
from jax.sharding import PartitionSpec as P

STEPS = 4
MESH = pl.DeviceIdType.MESH

lattice_velocities = (
    (0, 0, 0),
    (1, 0, 0),
    (-1, 0, 0),
    (0, 1, 0),
    (0, -1, 0),
    (0, 0, 1),
    (0, 0, -1),
    (1, 1, 0),
    (-1, -1, 0),
    (1, -1, 0),
    (-1, 1, 0),
    (1, 0, 1),
    (-1, 0, -1),
    (1, 0, -1),
    (-1, 0, 1),
    (0, 1, 1),
    (0, -1, -1),
    (0, 1, -1),
    (0, -1, 1),
)
relaxation = 1.25
bump_width = 0.15
level_offset = 0.05
LOG2E = math.log2(math.e)
SCALE = math.sqrt(LOG2E) / bump_width

COUNT = len(lattice_velocities)
ORDER = (
    [n for n in range(COUNT) if lattice_velocities[n][0] == 1]
    + [n for n in range(COUNT) if lattice_velocities[n][0] == -1]
    + [n for n in range(COUNT) if lattice_velocities[n][0] == 0]
)
SLOT = {number: place for place, number in enumerate(ORDER)}
UP_Y = [n for n in range(COUNT) if lattice_velocities[n][1] == 1]
DOWN_Y = [n for n in range(COUNT) if lattice_velocities[n][1] == -1]
CROSS = len(UP_Y)
CORNERS = [n for n in range(COUNT) if lattice_velocities[n][0] and lattice_velocities[n][1]]
PAIRS = [(n, n + 1) for n in range(1, COUNT, 2)]
LOW = 8
ROWS = 8


def add_all(values):
    while len(values) > 1:
        paired = [a + b for a, b in zip(values[0::2], values[1::2])]
        values = paired + ([values[-1]] if len(values) % 2 else [])
    return values[0]


def moments(field):
    diffs = {}
    sums = [field[0]]
    for plus, minus in PAIRS:
        sums.append(field[plus] + field[minus])
        diffs[plus] = field[plus] - field[minus]
    momentum = []
    for axis in range(3):
        total = diffs[1 + 2 * axis]
        for plus, _ in PAIRS[3:]:
            factor = lattice_velocities[plus][axis]
            if factor == 1:
                total = total + diffs[plus]
            elif factor == -1:
                total = total - diffs[plus]
        momentum.append(total)
    return add_all(sums), momentum


def collide(field):
    density, momentum = moments(field)
    inverse = 1.0 / density
    square = momentum[0] * momentum[0] + momentum[1] * momentum[1] + momentum[2] * momentum[2]
    even = density - 1.5 * (square * inverse)
    keep = 1.0 - relaxation
    result = [keep * field[0] + (relaxation / 3.0) * even] + [None] * (COUNT - 1)
    parts = {}
    for divisor in (18.0, 36.0):
        parts[divisor] = ((relaxation / divisor) * even, (relaxation * 4.5 / divisor) * inverse)
    for plus, minus in PAIRS:
        project = None
        for axis in range(3):
            factor = lattice_velocities[plus][axis]
            if factor:
                if project is None:
                    project = momentum[axis]
                elif factor == 1:
                    project = project + momentum[axis]
                else:
                    project = project - momentum[axis]
        divisor = 18.0 if plus < 7 else 36.0
        base, curve = parts[divisor]
        symmetric = base + curve * (project * project)
        odd = (3.0 * relaxation / divisor) * project
        result[plus] = keep * field[plus] + (symmetric + odd)
        result[minus] = keep * field[minus] + (symmetric - odd)
    return result


def kernel(
    sizes,
    f_hbm,
    par,
    direct,
    F,
    vort,
    img,
    A,
    B,
    E,
    SY,
    RY,
    SC,
    RC,
    U,
    VS,
    VR,
    L,
    PC,
    PA,
    PS,
    PR,
    in_sem,
    halo_s,
    halo_r,
    flow_s,
    flow_r,
    pa_s,
    pa_r,
    pr_s,
    pr_r,
):
    nd, ni, X, W, NZ, bumps = sizes
    d = lax.axis_index("depth")
    i = lax.axis_index("image")
    halves = W // ROWS
    ratio = ni // nd
    chunks = 4
    step_x = X // chunks

    loads = [
        pltpu.make_async_copy(
            f_hbm.at[:, pl.ds(c * step_x, step_x)],
            F.at[:, pl.ds(c * step_x, step_x)],
            in_sem.at[c],
        )
        for c in range(chunks)
    ]
    for copy in loads:
        copy.start()

    barrier = pltpu.get_barrier_semaphore()
    everyone = nd * ni
    me = d * ni + i

    def greet(offset, carry):
        other = lax.rem(me + offset, everyone)
        pl.semaphore_signal(
            barrier,
            inc=1,
            device_id={"depth": other // ni, "image": lax.rem(other, ni)},
            device_id_type=MESH,
        )
        return carry

    lax.fori_loop(1, everyone, greet, 0)

    ray = X * nd
    lane = lax.broadcasted_iota(jnp.int32, (8, NZ), 1)
    entries = jnp.full((8, NZ), direct[0].astype(jnp.float32), jnp.float32)
    for k in range(bumps):
        for kind in range(5):
            factor = SCALE if kind == 0 else (LOG2E / ray if kind == 1 else 1.0)
            entries = jnp.where(lane == kind * bumps + k, par[kind, 0, k] * factor, entries)
    PC[i] = entries

    def to(cx, cy):
        return {"depth": lax.rem(d + cx + nd, nd), "image": lax.rem(i + cy + ni, ni)}

    def remote(src, dst, send, recv, target):
        return pltpu.make_async_remote_copy(
            src_ref=src,
            dst_ref=dst,
            send_sem=send,
            recv_sem=recv,
            device_id=target,
            device_id_type=MESH,
        )

    starts = list(range(1, W - 1 - ROWS, ROWS)) + [W - 1 - ROWS]
    edge_rows = (0, W - 1)
    outward = (DOWN_Y, UP_Y)
    inward = (UP_Y, DOWN_Y)

    def pack(b, x, start, values):
        if start == 1:
            for number in DOWN_Y:
                E[b, 0, SLOT[number], pl.ds(ROWS + x, 1), :] = values[number][0:1]
        if start == W - 1 - ROWS:
            for number in UP_Y:
                E[b, 1, SLOT[number], pl.ds(ROWS + x, 1), :] = values[number][ROWS - 1 : ROWS]

    def streamed(S, x, start):
        field = []
        for number in range(COUNT):
            cx, cy, cz = lattice_velocities[number]
            value = S[SLOT[number], x + 1 - cx, pl.ds(LOW + start - cy, ROWS), :]
            if cz:
                value = pltpu.roll(value, cz % NZ, 1)
            field.append(value)
        return field

    def edge_streamed(b, side, x):
        field = []
        for number in range(COUNT):
            cx, _, cz = lattice_velocities[number]
            rows = slice(ROWS + x - cx, 2 * ROWS + x - cx)
            if number in inward[side]:
                value = RY[b, side, inward[side].index(number), rows, :]
            else:
                value = E[b, side, SLOT[number], rows, :]
            if cz:
                value = pltpu.roll(value, cz % NZ, 1)
            field.append(value)
        return field

    def update(S, D, b, x):
        for start in starts:
            values = collide(streamed(S, x, start))
            for number in range(COUNT):
                D[SLOT[number], x + 1, pl.ds(LOW + start, ROWS), :] = values[number]
            pack(b, x, start, values)

    def put_edges(D, b, side, x, values):
        row = LOW + edge_rows[side]
        for number in range(COUNT):
            cx, cy, _ = lattice_velocities[number]
            value = values[number]
            if number in inward[side]:
                for r in range(ROWS):
                    D[SLOT[number], x + r + 1, row : row + 1, :] = value[r : r + 1]
                continue
            if cy == 0:
                E[b, side, SLOT[number], ROWS + x : 2 * ROWS + x, :] = value
            else:
                SY[side, outward[side].index(number), x : x + ROWS, :] = value
            if cx == 1 and x == X - ROWS:
                D[SLOT[number], X, row : row + 1, :] = value[ROWS - 1 : ROWS]
            if cx == -1 and x == 0:
                D[SLOT[number], 1, row : row + 1, :] = value[0:1]

    inner = pl.ds(LOW, W)

    def exchange(D, turn):
        slot = turn % 2
        for k, number in enumerate(CORNERS):
            cx, cy, _ = lattice_velocities[number]
            side = 1 if cy == 1 else 0
            edge = X - 1 if cx == 1 else 0
            SC[k, 0:1, :] = SY[side, outward[side].index(number), edge : edge + 1, :]
        copies = []

        def add(src, dst, target):
            k = len(copies)
            copies.append(remote(src, dst, halo_s.at[turn, k], halo_r.at[turn, k], target))

        body = pl.ds(ROWS, X)
        add(SY.at[1], RY.at[slot, 0, :, body], to(0, 1))
        add(SY.at[0], RY.at[slot, 1, :, body], to(0, -1))
        for k, number in enumerate(CORNERS):
            cx, cy, _ = lattice_velocities[number]
            add(SC.at[k], RC.at[slot, k], to(cx, cy))
        add(D.at[pl.ds(0, CROSS), X, inner], D.at[pl.ds(0, CROSS), 0, inner], to(1, 0))
        add(D.at[pl.ds(CROSS, CROSS), 1, inner], D.at[pl.ds(CROSS, CROSS), X + 1, inner], to(-1, 0))
        for copy in copies:
            copy.start()
        return copies

    def finish(copies, D, turn):
        slot = turn % 2
        for copy in copies:
            copy.wait()
        for number in range(COUNT):
            cx, cy, _ = lattice_velocities[number]
            if cx == 0:
                continue
            plane, place = (0, ROWS - 1) if cx == 1 else (X + 1, ROWS + X)
            for side in range(2):
                if number in inward[side]:
                    k = CORNERS.index(number)
                    j = inward[side].index(number)
                    RY[slot, side, j, place : place + 1, :] = RC[slot, k, 0:1, :]
                else:
                    row = LOW + edge_rows[side] - cy
                    E[slot, side, SLOT[number], place : place + 1, :] = D[
                        SLOT[number], plane, row : row + 1, :
                    ]

    def first(x, carry):
        for h in range(halves):
            field = [F[number, x, pl.ds(ROWS * h, ROWS), :] for number in range(COUNT)]
            values = collide(field)
            for number in range(COUNT):
                A[SLOT[number], x + 1, pl.ds(LOW + ROWS * h, ROWS), :] = values[number]
            for side, edge in ((0, 0), (1, ROWS - 1)):
                if h != (0 if side == 0 else halves - 1):
                    continue
                near = 1 if side == 0 else ROWS - 2
                for number in range(COUNT):
                    if lattice_velocities[number][1] == 0:
                        E[0, side, SLOT[number], pl.ds(ROWS + x, 1), :] = values[number][
                            edge : edge + 1
                        ]
                for j, number in enumerate(outward[side]):
                    SY[side, j, pl.ds(x, 1), :] = values[number][edge : edge + 1]
                    E[0, side, SLOT[number], pl.ds(ROWS + x, 1), :] = values[number][
                        near : near + 1
                    ]
        return carry

    for c in range(chunks):
        loads[c].wait()
        lax.fori_loop(c * step_x, (c + 1) * step_x, first, 0)

    pl.semaphore_wait(barrier, everyone - 1)
    shares = [
        remote(PC.at[i], PC.at[i], pa_s.at[o], pa_r.at[o], to(0, o)) for o in range(1, ni)
    ]
    copies = exchange(A, 0)
    for copy in shares:
        copy.start()

    source, target = A, B
    for turn in range(1, STEPS):

        def middle(x, carry, source=source, target=target, turn=turn):
            update(source, target, turn % 2, x)
            return carry

        lax.fori_loop(1, X - 1, middle, 0)
        finish(copies, source, turn - 1)
        for x in (0, X - 1):
            middle(x, 0)
        for side in range(2):
            for x in range(0, X, ROWS):
                put_edges(target, turn % 2, side, x, collide(edge_streamed((turn - 1) % 2, side, x)))
        copies = exchange(target, turn)
        source, target = target, source

    def flow_of(field):
        density, momentum = moments(field)
        inverse = 1.0 / density
        return [momentum[axis] * inverse for axis in (1, 2, 0)]

    def last(x, carry):
        for start in starts:
            field = streamed(source, x, start)
            for number in range(COUNT):
                F[number, x, pl.ds(start, ROWS), :] = field[number]
            for place, value in enumerate(flow_of(field)):
                U[place, x + 1, pl.ds(LOW + start, ROWS), :] = value
        return carry

    lax.fori_loop(1, X - 1, last, 0)
    finish(copies, source, STEPS - 1)
    for x in (0, X - 1):
        last(x, 0)
    for side in range(2):
        row = edge_rows[side]
        for x in range(0, X, ROWS):
            field = edge_streamed((STEPS - 1) % 2, side, x)
            for number in range(COUNT):
                for r in range(ROWS):
                    F[number, x + r, row : row + 1, :] = field[number][r : r + 1]
            flow = flow_of(field)
            for place, value in enumerate(flow):
                for r in range(ROWS):
                    U[place, x + r + 1, LOW + row : LOW + row + 1, :] = value[r : r + 1]
            VS[side, 0, x : x + ROWS, :] = flow[1]
            VS[side, 1, x : x + ROWS, :] = flow[2]
    flows = [
        remote(VS.at[1], VR.at[1], flow_s.at[0], flow_r.at[0], to(0, 1)),
        remote(VS.at[0], VR.at[0], flow_s.at[1], flow_r.at[1], to(0, -1)),
        remote(
            U.at[pl.ds(0, 2), X, inner],
            U.at[pl.ds(0, 2), 0, inner],
            flow_s.at[2],
            flow_r.at[2],
            to(1, 0),
        ),
        remote(
            U.at[pl.ds(0, 2), 1, inner],
            U.at[pl.ds(0, 2), X + 1, inner],
            flow_s.at[3],
            flow_r.at[3],
            to(-1, 0),
        ),
    ]
    for copy in flows:
        copy.start()
    for copy in shares:
        copy.wait()

    def expand(m, carry):
        for block in range(PA.shape[1] // 8):
            line = lax.broadcasted_iota(jnp.int32, (8, NZ), 0) + 8 * block
            chosen = jnp.where(lane == line, PC[m], 0.0)
            value = jnp.sum(chosen, axis=1, keepdims=True)
            PA[m, pl.ds(8 * block, 8), :] = jnp.broadcast_to(value, (8, NZ))
        return carry

    lax.fori_loop(0, ni, expand, 0)
    for copy in flows:
        copy.wait()

    def flow_rows(x, carry):
        for place, j in ((1, 0), (2, 1)):
            U[place, x + 1, pl.ds(LOW - 1, 1), :] = VR[1, j, pl.ds(x, 1), :]
            U[place, x + 1, pl.ds(LOW + W, 1), :] = VR[0, j, pl.ds(x, 1), :]
        return carry

    lax.fori_loop(0, X, flow_rows, 0)

    def spin(x, carry):
        def across_x(place):
            return (U[place, x + 2, inner, :] - U[place, x, inner, :]) * 0.5

        def across_y(place):
            above = U[place, x + 1, pl.ds(LOW + 1, W), :]
            return (above - U[place, x + 1, pl.ds(LOW - 1, W), :]) * 0.5

        def across_z(place):
            value = U[place, x + 1, inner, :]
            return (pltpu.roll(value, NZ - 1, 1) - pltpu.roll(value, 1, 1)) * 0.5

        spin_x = across_y(1) - across_z(0)
        spin_y = across_z(2) - across_x(1)
        spin_z = across_x(0) - across_y(2)
        size = jnp.sqrt(spin_x * spin_x + spin_y * spin_y + spin_z * spin_z)
        rounded = size.astype(jnp.bfloat16)
        vort[x] = rounded
        value = rounded.astype(jnp.float32)
        L[x] = (value / (value + level_offset)) * SCALE
        return carry

    lax.fori_loop(0, X, spin, 0)

    owner = i // ratio
    mine = d * ratio + lax.rem(i, ratio)

    def row(m, r):
        return jnp.broadcast_to(PA[m, pl.ds(r, 1), :], (ROWS, NZ))

    def blend(backward, through, colors, local_through, local_colors):
        fade = jnp.where(backward, local_through, 1.0)
        lit = jnp.where(backward, 1.0, through)
        mixed = [color * fade + lit * local for color, local in zip(colors, local_colors)]
        return through * local_through, mixed

    def piece(o, m):
        return remote(
            PS.at[m],
            PR.at[mine],
            pr_s.at[o],
            pr_r.at[mine],
            {"depth": owner, "image": m},
        )

    def render(o, carry):
        m = lax.rem(i + 1 + o, ni)
        backward = row(m, 5 * bumps) > 0.5

        def along(x, state):
            new = []
            levels = [L[x, pl.ds(ROWS * h, ROWS), :] for h in range(halves)]
            totals = [[None] * 4 for h in range(halves)]
            for k in range(bumps):
                centre = row(m, k)
                gains = [row(m, (1 + j) * bumps + k) for j in range(4)]
                for h in range(halves):
                    offset = levels[h] - centre
                    bump = jnp.exp2(-(offset * offset))
                    for j in range(4):
                        term = gains[j] * bump
                        totals[h][j] = term if k == 0 else totals[h][j] + term
            for h in range(halves):
                through, colors = state[4 * h], state[4 * h + 1 : 4 * h + 4]
                local = jnp.exp2(-totals[h][0])
                alpha = 1.0 - local
                shades = [alpha * total for total in totals[h][1:]]
                through, colors = blend(backward, through, colors, local, shades)
                new += [through] + list(colors)
            return tuple(new)

        zero = jnp.zeros((ROWS, NZ), jnp.float32)
        start = (jnp.ones((ROWS, NZ), jnp.float32), zero, zero, zero) * halves
        state = lax.fori_loop(0, X, along, start)
        for h in range(halves):
            through, colors = state[4 * h], state[4 * h + 1 : 4 * h + 4]
            for j, value in enumerate(list(colors) + [through]):
                PS[m, j, pl.ds(ROWS * h, ROWS), :] = value
        local_target = jnp.logical_and(owner == d, m == i)

        @pl.when(local_target)
        def _():
            PR[mine] = PS[m]

        @pl.when(jnp.logical_not(local_target))
        def _():
            piece(o, m).start()

        return carry

    lax.fori_loop(0, ni, render, 0)

    def sent(o, carry):
        m = lax.rem(i + 1 + o, ni)

        @pl.when(jnp.logical_not(jnp.logical_and(owner == d, m == i)))
        def _():
            piece(o, m).wait_send()

        return carry

    def arrived(slot, carry):
        @pl.when(jnp.logical_not(jnp.logical_and(owner == d, slot == mine)))
        def _():
            remote(
                PS.at[0], PR.at[slot], pr_s.at[0], pr_r.at[slot], {"depth": d, "image": i}
            ).wait_recv()

        return carry

    lax.fori_loop(0, nd * ratio, arrived, 0)
    backward = row(i, 5 * bumps) > 0.5
    for part in range(ratio):
        for h in range(halves):
            rows = pl.ds(ROWS * h, ROWS)
            through = jnp.ones((ROWS, NZ), jnp.float32)
            colors = [jnp.zeros((ROWS, NZ), jnp.float32)] * 3
            for slab in range(nd):
                slot = slab * ratio + part
                local = [PR[slot, j, rows, :] for j in range(4)]
                through, colors = blend(backward, through, colors, local[3], local[:3])
            for j, value in enumerate(colors + [1.0 - through]):
                img[0, j, pl.ds(part * W + ROWS * h, ROWS), :] = value
    lax.fori_loop(0, ni, sent, 0)


def on_device(populations, transfer, direction):
    nd, ni = lax.axis_size("depth"), lax.axis_size("image")
    count, X, W, NZ = populations.shape
    bumps = transfer.shape[2]
    assert transfer.shape[0] == 1 and ni % nd == 0 and W % ROWS == 0 and W >= 2 * ROWS and X % 8 == 0
    sizes = (nd, ni, X, W, NZ, bumps)
    ratio = ni // nd
    padded = W + 2 * ROWS
    f32 = jnp.float32
    table = -(-(5 * bumps + 1) // 8) * 8
    dma = pltpu.SemaphoreType.DMA
    return pl.pallas_call(
        functools.partial(kernel, sizes),
        out_shape=(
            pltpu.VMEM(populations.shape, f32),
            jax.ShapeDtypeStruct((X, W, NZ), jnp.bfloat16),
            jax.ShapeDtypeStruct((1, 4, ratio * W, NZ), f32),
        ),
        in_specs=[
            pl.BlockSpec(memory_space=pl.ANY),
            pl.BlockSpec(memory_space=pltpu.SMEM),
            pl.BlockSpec(memory_space=pltpu.SMEM),
        ],
        out_specs=(
            pl.BlockSpec(memory_space=pltpu.VMEM),
            pl.BlockSpec(memory_space=pltpu.VMEM),
            pl.BlockSpec(memory_space=pltpu.VMEM),
        ),
        scratch_shapes=[
            pltpu.VMEM((COUNT, X + 2, padded, NZ), f32),
            pltpu.VMEM((COUNT, X + 2, padded, NZ), f32),
            pltpu.VMEM((2, 2, COUNT, X + 2 * ROWS, NZ), f32),
            pltpu.VMEM((2, CROSS, X, NZ), f32),
            pltpu.VMEM((2, 2, CROSS, X + 2 * ROWS, NZ), f32),
            pltpu.VMEM((4, 8, NZ), f32),
            pltpu.VMEM((2, 4, 8, NZ), f32),
            pltpu.VMEM((3, X + 2, padded, NZ), f32),
            pltpu.VMEM((2, 2, X, NZ), f32),
            pltpu.VMEM((2, 2, X, NZ), f32),
            pltpu.VMEM((X, W, NZ), f32),
            pltpu.VMEM((ni, 8, NZ), f32),
            pltpu.VMEM((ni, table, NZ), f32),
            pltpu.VMEM((ni, 4, W, NZ), f32),
            pltpu.VMEM((nd * ratio, 4, W, NZ), f32),
            dma((4,)),
            dma((STEPS, 8)),
            dma((STEPS, 8)),
            dma((4,)),
            dma((4,)),
            dma((ni,)),
            dma((ni,)),
            dma((ni,)),
            dma((nd * ratio,)),
        ],
        compiler_params=pltpu.CompilerParams(
            collective_id=0, has_side_effects=True, vmem_limit_bytes=56 << 20
        ),
    )(populations, transfer.transpose(1, 0, 2), direction)


def solution(mesh):
    in_specs = (P(None, "depth", "image", None), P("image", None, None), P("image"))
    out_specs = (
        P(None, "depth", "image", None),
        P("depth", "image", None),
        P("image", None, "depth", None),
    )
    return jax.shard_map(
        on_device, mesh=mesh, in_specs=in_specs, out_specs=out_specs, check_vma=False
    )
```

```python
import functools
import math

import jax
import jax.numpy as jnp
from jax import lax
from jax.experimental import pallas as pl
from jax.experimental.pallas import tpu as pltpu
from jax.sharding import PartitionSpec as P

STEPS = 4
MESH = pl.DeviceIdType.MESH

lattice_velocities = (
    (0, 0, 0),
    (1, 0, 0),
    (-1, 0, 0),
    (0, 1, 0),
    (0, -1, 0),
    (0, 0, 1),
    (0, 0, -1),
    (1, 1, 0),
    (-1, -1, 0),
    (1, -1, 0),
    (-1, 1, 0),
    (1, 0, 1),
    (-1, 0, -1),
    (1, 0, -1),
    (-1, 0, 1),
    (0, 1, 1),
    (0, -1, -1),
    (0, 1, -1),
    (0, -1, 1),
)
relaxation = 1.25
bump_width = 0.15
level_offset = 0.05
LOG2E = math.log2(math.e)
SCALE = math.sqrt(LOG2E) / bump_width

COUNT = len(lattice_velocities)
ORDER = (
    [n for n in range(COUNT) if lattice_velocities[n][0] == 1]
    + [n for n in range(COUNT) if lattice_velocities[n][0] == -1]
    + [n for n in range(COUNT) if lattice_velocities[n][0] == 0]
)
SLOT = {number: place for place, number in enumerate(ORDER)}
UP_Y = [n for n in range(COUNT) if lattice_velocities[n][1] == 1]
DOWN_Y = [n for n in range(COUNT) if lattice_velocities[n][1] == -1]
CROSS = len(UP_Y)
CORNERS = [n for n in range(COUNT) if lattice_velocities[n][0] and lattice_velocities[n][1]]
PAIRS = [(n, n + 1) for n in range(1, COUNT, 2)]
LOW = 8
ROWS = 8


def add_all(values):
    while len(values) > 1:
        paired = [a + b for a, b in zip(values[0::2], values[1::2])]
        values = paired + ([values[-1]] if len(values) % 2 else [])
    return values[0]


def moments(field):
    diffs = {}
    sums = [field[0]]
    for plus, minus in PAIRS:
        sums.append(field[plus] + field[minus])
        diffs[plus] = field[plus] - field[minus]
    momentum = []
    for axis in range(3):
        total = diffs[1 + 2 * axis]
        for plus, _ in PAIRS[3:]:
            factor = lattice_velocities[plus][axis]
            if factor == 1:
                total = total + diffs[plus]
            elif factor == -1:
                total = total - diffs[plus]
        momentum.append(total)
    return add_all(sums), momentum


def collide(field):
    density, momentum = moments(field)
    inverse = 1.0 / density
    square = momentum[0] * momentum[0] + momentum[1] * momentum[1] + momentum[2] * momentum[2]
    even = density - 1.5 * (square * inverse)
    keep = 1.0 - relaxation
    result = [keep * field[0] + (relaxation / 3.0) * even] + [None] * (COUNT - 1)
    parts = {}
    for divisor in (18.0, 36.0):
        parts[divisor] = ((relaxation / divisor) * even, (relaxation * 4.5 / divisor) * inverse)
    for plus, minus in PAIRS:
        project = None
        for axis in range(3):
            factor = lattice_velocities[plus][axis]
            if factor:
                if project is None:
                    project = momentum[axis]
                elif factor == 1:
                    project = project + momentum[axis]
                else:
                    project = project - momentum[axis]
        divisor = 18.0 if plus < 7 else 36.0
        base, curve = parts[divisor]
        symmetric = base + curve * (project * project)
        odd = (3.0 * relaxation / divisor) * project
        result[plus] = keep * field[plus] + (symmetric + odd)
        result[minus] = keep * field[minus] + (symmetric - odd)
    return result


def kernel(
    sizes,
    f_hbm,
    par,
    direct,
    F,
    vort,
    img,
    A,
    B,
    E,
    SY,
    RY,
    SC,
    RC,
    U,
    VS,
    VR,
    L,
    G,
    PC,
    PA,
    PS,
    PR,
    in_sem,
    halo_s,
    halo_r,
    flow_s,
    flow_r,
    pa_s,
    pa_r,
    pr_s,
    pr_r,
):
    nd, ni, X, W, NZ, bumps = sizes
    d = lax.axis_index("depth")
    i = lax.axis_index("image")
    halves = W // ROWS
    ratio = ni // nd
    chunks = 4
    step_x = X // chunks

    loads = [
        pltpu.make_async_copy(
            f_hbm.at[:, pl.ds(c * step_x, step_x)],
            F.at[:, pl.ds(c * step_x, step_x)],
            in_sem.at[c],
        )
        for c in range(chunks)
    ]
    for copy in loads:
        copy.start()

    barrier = pltpu.get_barrier_semaphore()
    everyone = nd * ni
    me = d * ni + i

    def greet(offset, carry):
        other = lax.rem(me + offset, everyone)
        pl.semaphore_signal(
            barrier,
            inc=1,
            device_id={"depth": other // ni, "image": lax.rem(other, ni)},
            device_id_type=MESH,
        )
        return carry

    lax.fori_loop(1, everyone, greet, 0)

    ray = X * nd
    lane = lax.broadcasted_iota(jnp.int32, (8, NZ), 1)
    entries = jnp.full((8, NZ), direct[0].astype(jnp.float32), jnp.float32)
    for k in range(bumps):
        for kind in range(5):
            factor = SCALE if kind == 0 else (LOG2E / ray if kind == 1 else 1.0)
            entries = jnp.where(lane == kind * bumps + k, par[kind, 0, k] * factor, entries)
    gain = pltpu.roll(entries, bumps, 1)
    shift = gain * gain - jnp.log2(entries)
    ratios = entries / gain
    for kind in (3, 4):
        ratios = jnp.where(
            lane < kind * bumps, ratios, entries / pltpu.roll(entries, (kind - 1) * bumps, 1)
        )
    table = jnp.where(lane < 2 * bumps, shift, ratios)
    table = jnp.where(lane < bumps, 2.0 * entries, table)
    PC[i] = jnp.where(lane < 5 * bumps, table, entries)[0:1]

    def to(cx, cy):
        return {"depth": lax.rem(d + cx + nd, nd), "image": lax.rem(i + cy + ni, ni)}

    def remote(src, dst, send, recv, target):
        return pltpu.make_async_remote_copy(
            src_ref=src,
            dst_ref=dst,
            send_sem=send,
            recv_sem=recv,
            device_id=target,
            device_id_type=MESH,
        )

    starts = list(range(1, W - 1 - ROWS, ROWS)) + [W - 1 - ROWS]
    edge_rows = (0, W - 1)
    outward = (DOWN_Y, UP_Y)
    inward = (UP_Y, DOWN_Y)

    def pack(b, x, start, values):
        if start == 1:
            for number in DOWN_Y:
                E[b, 0, SLOT[number], pl.ds(ROWS + x, 1), :] = values[number][0:1]
        if start == W - 1 - ROWS:
            for number in UP_Y:
                E[b, 1, SLOT[number], pl.ds(ROWS + x, 1), :] = values[number][ROWS - 1 : ROWS]

    def streamed(S, x, start):
        field = []
        for number in range(COUNT):
            cx, cy, cz = lattice_velocities[number]
            value = S[SLOT[number], x + 1 - cx, pl.ds(LOW + start - cy, ROWS), :]
            if cz:
                value = pltpu.roll(value, cz % NZ, 1)
            field.append(value)
        return field

    def edge_streamed(b, side, x):
        field = []
        for number in range(COUNT):
            cx, _, cz = lattice_velocities[number]
            rows = slice(ROWS + x - cx, 2 * ROWS + x - cx)
            if number in inward[side]:
                value = RY[b, side, inward[side].index(number), rows, :]
            else:
                value = E[b, side, SLOT[number], rows, :]
            if cz:
                value = pltpu.roll(value, cz % NZ, 1)
            field.append(value)
        return field

    def update(S, D, b, x):
        for start in starts:
            values = collide(streamed(S, x, start))
            for number in range(COUNT):
                D[SLOT[number], x + 1, pl.ds(LOW + start, ROWS), :] = values[number]
            pack(b, x, start, values)

    def put_edges(D, b, side, x, values):
        row = LOW + edge_rows[side]
        for number in range(COUNT):
            cx, cy, _ = lattice_velocities[number]
            value = values[number]
            if number in inward[side]:
                for r in range(ROWS):
                    D[SLOT[number], x + r + 1, row : row + 1, :] = value[r : r + 1]
                continue
            if cy == 0:
                E[b, side, SLOT[number], ROWS + x : 2 * ROWS + x, :] = value
            else:
                SY[side, outward[side].index(number), x : x + ROWS, :] = value
            if cx == 1 and x == X - ROWS:
                D[SLOT[number], X, row : row + 1, :] = value[ROWS - 1 : ROWS]
            if cx == -1 and x == 0:
                D[SLOT[number], 1, row : row + 1, :] = value[0:1]

    inner = pl.ds(LOW, W)

    def exchange(D, turn, columns=None):
        slot = turn % 2
        for k, number in enumerate(CORNERS):
            cx, cy, _ = lattice_velocities[number]
            side = 1 if cy == 1 else 0
            edge = X - 1 if cx == 1 else 0
            SC[k] = SY[side, outward[side].index(number), edge : edge + 1, :]
        copies = []

        def add(src, dst, target):
            k = len(copies)
            copies.append(remote(src, dst, halo_s.at[turn, k], halo_r.at[turn, k], target))
            copies[-1].start()

        body = pl.ds(ROWS, X)
        add(SY.at[1], RY.at[slot, 0, :, body], to(0, 1))
        add(SY.at[0], RY.at[slot, 1, :, body], to(0, -1))
        for k, number in enumerate(CORNERS):
            cx, cy, _ = lattice_velocities[number]
            add(SC.at[k], RC.at[slot, k], to(cx, cy))
        if columns is not None:
            for x in (0, X - 1):
                columns(x, 0)
        add(D.at[pl.ds(0, CROSS), X, inner], D.at[pl.ds(0, CROSS), 0, inner], to(1, 0))
        add(D.at[pl.ds(CROSS, CROSS), 1, inner], D.at[pl.ds(CROSS, CROSS), X + 1, inner], to(-1, 0))
        return copies

    def finish(copies, D, turn):
        slot = turn % 2
        for copy in copies:
            copy.wait()
        for number in range(COUNT):
            cx, cy, _ = lattice_velocities[number]
            if cx == 0:
                continue
            plane, place = (0, ROWS - 1) if cx == 1 else (X + 1, ROWS + X)
            for side in range(2):
                if number in inward[side]:
                    k = CORNERS.index(number)
                    j = inward[side].index(number)
                    RY[slot, side, j, place : place + 1, :] = RC[slot, k]
                else:
                    row = LOW + edge_rows[side] - cy
                    E[slot, side, SLOT[number], place : place + 1, :] = D[
                        SLOT[number], plane, row : row + 1, :
                    ]

    def first(x, carry):
        for h in range(halves):
            field = [F[number, x, pl.ds(ROWS * h, ROWS), :] for number in range(COUNT)]
            values = collide(field)
            for number in range(COUNT):
                A[SLOT[number], x + 1, pl.ds(LOW + ROWS * h, ROWS), :] = values[number]
            for side, edge in ((0, 0), (1, ROWS - 1)):
                if h != (0 if side == 0 else halves - 1):
                    continue
                near = 1 if side == 0 else ROWS - 2
                for number in range(COUNT):
                    if lattice_velocities[number][1] == 0:
                        E[0, side, SLOT[number], pl.ds(ROWS + x, 1), :] = values[number][
                            edge : edge + 1
                        ]
                for j, number in enumerate(outward[side]):
                    SY[side, j, pl.ds(x, 1), :] = values[number][edge : edge + 1]
                    E[0, side, SLOT[number], pl.ds(ROWS + x, 1), :] = values[number][
                        near : near + 1
                    ]
        return carry

    for c in range(chunks):
        loads[c].wait()
        lax.fori_loop(c * step_x, (c + 1) * step_x, first, 0)

    pl.semaphore_wait(barrier, everyone - 1)
    shares = [
        remote(PC.at[i], PC.at[i], pa_s.at[o], pa_r.at[o], to(0, o)) for o in range(1, ni)
    ]
    copies = exchange(A, 0)
    for copy in shares:
        copy.start()

    source, target = A, B
    for turn in range(1, STEPS):

        def middle(x, carry, source=source, target=target, turn=turn):
            update(source, target, turn % 2, x)
            return carry

        lax.fori_loop(1, X - 1, middle, 0)
        finish(copies, source, turn - 1)
        for side in range(2):
            for x in range(0, X, ROWS):
                put_edges(target, turn % 2, side, x, collide(edge_streamed((turn - 1) % 2, side, x)))
        copies = exchange(target, turn, middle)
        source, target = target, source

    def flow_of(field):
        density, momentum = moments(field)
        inverse = 1.0 / density
        return [momentum[axis] * inverse for axis in (1, 2, 0)]

    def last(x, carry):
        for start in starts:
            field = streamed(source, x, start)
            for number in range(COUNT):
                F[number, x, pl.ds(start, ROWS), :] = field[number]
            for place, value in enumerate(flow_of(field)):
                U[place, x + 1, pl.ds(LOW + start, ROWS), :] = value
        return carry

    lax.fori_loop(1, X - 1, last, 0)
    finish(copies, source, STEPS - 1)
    for x in (0, X - 1):
        last(x, 0)
    for side in range(2):
        row = edge_rows[side]
        for x in range(0, X, ROWS):
            field = edge_streamed((STEPS - 1) % 2, side, x)
            flow = flow_of(field)
            for place, value in enumerate(flow):
                for r in range(ROWS):
                    U[place, x + r + 1, LOW + row : LOW + row + 1, :] = value[r : r + 1]
            VS[side, 0, x : x + ROWS, :] = flow[1]
            VS[side, 1, x : x + ROWS, :] = flow[2]
    flows = [
        remote(VS.at[1], VR.at[1], flow_s.at[0], flow_r.at[0], to(0, 1)),
        remote(VS.at[0], VR.at[0], flow_s.at[1], flow_r.at[1], to(0, -1)),
        remote(
            U.at[pl.ds(0, 2), X, inner],
            U.at[pl.ds(0, 2), 0, inner],
            flow_s.at[2],
            flow_r.at[2],
            to(1, 0),
        ),
        remote(
            U.at[pl.ds(0, 2), 1, inner],
            U.at[pl.ds(0, 2), X + 1, inner],
            flow_s.at[3],
            flow_r.at[3],
            to(-1, 0),
        ),
    ]
    for copy in flows:
        copy.start()
    for side in range(2):
        row = edge_rows[side]
        for x in range(0, X, ROWS):
            field = edge_streamed((STEPS - 1) % 2, side, x)
            for number in range(COUNT):
                for r in range(ROWS):
                    F[number, x + r, row : row + 1, :] = field[number][r : r + 1]
    for copy in shares:
        copy.wait()

    def expand(m, carry):
        for block in range(PA.shape[1] // 8):
            line = lax.broadcasted_iota(jnp.int32, (8, NZ), 0) + 8 * block
            chosen = jnp.where(lane == line, jnp.broadcast_to(PC[m], (8, NZ)), 0.0)
            value = jnp.sum(chosen, axis=1, keepdims=True)
            PA[m, pl.ds(8 * block, 8), :] = jnp.broadcast_to(value, (8, NZ))
        return carry

    lax.fori_loop(0, ni, expand, 0)
    for copy in flows:
        copy.wait()

    def flow_rows(x, carry):
        for place, j in ((1, 0), (2, 1)):
            U[place, x + 1, pl.ds(LOW - 1, 1), :] = VR[1, j, pl.ds(x, 1), :]
            U[place, x + 1, pl.ds(LOW + W, 1), :] = VR[0, j, pl.ds(x, 1), :]
        return carry

    lax.fori_loop(0, X, flow_rows, 0)

    def spin(x, carry):
        def across_x(place):
            return (U[place, x + 2, inner, :] - U[place, x, inner, :]) * 0.5

        def across_y(place):
            above = U[place, x + 1, pl.ds(LOW + 1, W), :]
            return (above - U[place, x + 1, pl.ds(LOW - 1, W), :]) * 0.5

        def across_z(place):
            value = U[place, x + 1, inner, :]
            return (pltpu.roll(value, NZ - 1, 1) - pltpu.roll(value, 1, 1)) * 0.5

        spin_x = across_y(1) - across_z(0)
        spin_y = across_z(2) - across_x(1)
        spin_z = across_x(0) - across_y(2)
        size = jnp.sqrt(spin_x * spin_x + spin_y * spin_y + spin_z * spin_z)
        rounded = size.astype(jnp.bfloat16)
        vort[x] = rounded
        value = rounded.astype(jnp.float32)
        level = (value / (value + level_offset)) * SCALE
        L[x] = level
        G[x] = jnp.exp2(-(level * level))
        return carry

    lax.fori_loop(0, X, spin, 0)

    owner = i // ratio
    mine = d * ratio + lax.rem(i, ratio)

    def row(m, r):
        return jnp.broadcast_to(PA[m, pl.ds(r, 1), :], (ROWS, NZ))

    def blend(backward, through, colors, local_through, local_colors):
        fade = jnp.where(backward, local_through, 1.0)
        lit = jnp.where(backward, 1.0, through)
        mixed = [color * fade + lit * local for color, local in zip(colors, local_colors)]
        return through * local_through, mixed

    def piece(o, m):
        return remote(
            PS.at[m],
            PR.at[mine],
            pr_s.at[o],
            pr_r.at[mine],
            {"depth": owner, "image": m},
        )

    def render(o, carry):
        m = lax.rem(i + 1 + o, ni)
        backward = row(m, 5 * bumps) > 0.5

        def along(x, state):
            new = []
            levels = [L[x, pl.ds(ROWS * h, ROWS), :] for h in range(halves)]
            totals = [[None] * 4 for h in range(halves)]
            for k in range(bumps):
                centre = row(m, k)
                shift = row(m, bumps + k)
                gains = [row(m, (1 + j) * bumps + k) for j in range(1, 4)]
                for h in range(halves):
                    bump = jnp.exp2(levels[h] * centre - shift)
                    for j in range(4):
                        term = gains[j - 1] * bump if j else bump
                        totals[h][j] = term if k == 0 else totals[h][j] + term
            for h in range(halves):
                through, colors = state[4 * h], state[4 * h + 1 : 4 * h + 4]
                common = G[x, pl.ds(ROWS * h, ROWS), :]
                optical = totals[h][0] * common
                local = jnp.exp2(-optical)
                alpha = (1.0 - local) * common
                shades = [alpha * total for total in totals[h][1:]]
                through, colors = blend(backward, through, colors, local, shades)
                new += [through] + list(colors)
            return tuple(new)

        zero = jnp.zeros((ROWS, NZ), jnp.float32)
        start = (jnp.ones((ROWS, NZ), jnp.float32), zero, zero, zero) * halves
        state = lax.fori_loop(0, X, along, start)
        for h in range(halves):
            through, colors = state[4 * h], state[4 * h + 1 : 4 * h + 4]
            for j, value in enumerate(list(colors) + [through]):
                PS[m, j, pl.ds(ROWS * h, ROWS), :] = value
        local_target = jnp.logical_and(owner == d, m == i)

        @pl.when(local_target)
        def _():
            PR[mine] = PS[m]

        @pl.when(jnp.logical_not(local_target))
        def _():
            piece(o, m).start()

        return carry

    lax.fori_loop(0, ni, render, 0)

    def sent(o, carry):
        m = lax.rem(i + 1 + o, ni)

        @pl.when(jnp.logical_not(jnp.logical_and(owner == d, m == i)))
        def _():
            piece(o, m).wait_send()

        return carry

    def arrived(slot, carry):
        @pl.when(jnp.logical_not(jnp.logical_and(owner == d, slot == mine)))
        def _():
            remote(
                PS.at[0], PR.at[slot], pr_s.at[0], pr_r.at[slot], {"depth": d, "image": i}
            ).wait_recv()

        return carry

    lax.fori_loop(0, nd * ratio, arrived, 0)
    backward = row(i, 5 * bumps) > 0.5
    for part in range(ratio):
        for h in range(halves):
            rows = pl.ds(ROWS * h, ROWS)
            through = jnp.ones((ROWS, NZ), jnp.float32)
            colors = [jnp.zeros((ROWS, NZ), jnp.float32)] * 3
            for slab in range(nd):
                slot = slab * ratio + part
                local = [PR[slot, j, rows, :] for j in range(4)]
                through, colors = blend(backward, through, colors, local[3], local[:3])
            for j, value in enumerate(colors + [1.0 - through]):
                img[0, j, pl.ds(part * W + ROWS * h, ROWS), :] = value
    lax.fori_loop(0, ni, sent, 0)


def on_device(populations, transfer, direction):
    nd, ni = lax.axis_size("depth"), lax.axis_size("image")
    count, X, W, NZ = populations.shape
    bumps = transfer.shape[2]
    assert transfer.shape[0] == 1 and ni % nd == 0 and W % ROWS == 0 and W >= 2 * ROWS and X % 8 == 0
    sizes = (nd, ni, X, W, NZ, bumps)
    ratio = ni // nd
    padded = W + 2 * ROWS
    f32 = jnp.float32
    table = -(-(5 * bumps + 1) // 8) * 8
    dma = pltpu.SemaphoreType.DMA
    return pl.pallas_call(
        functools.partial(kernel, sizes),
        out_shape=(
            pltpu.VMEM(populations.shape, f32),
            jax.ShapeDtypeStruct((X, W, NZ), jnp.bfloat16),
            jax.ShapeDtypeStruct((1, 4, ratio * W, NZ), f32),
        ),
        in_specs=[
            pl.BlockSpec(memory_space=pl.ANY),
            pl.BlockSpec(memory_space=pltpu.SMEM),
            pl.BlockSpec(memory_space=pltpu.SMEM),
        ],
        out_specs=(
            pl.BlockSpec(memory_space=pltpu.VMEM),
            pl.BlockSpec(memory_space=pltpu.VMEM),
            pl.BlockSpec(memory_space=pltpu.VMEM),
        ),
        scratch_shapes=[
            pltpu.VMEM((COUNT, X + 2, padded, NZ), f32),
            pltpu.VMEM((COUNT, X + 2, padded, NZ), f32),
            pltpu.VMEM((2, 2, COUNT, X + 2 * ROWS, NZ), f32),
            pltpu.VMEM((2, CROSS, X, NZ), f32),
            pltpu.VMEM((2, 2, CROSS, X + 2 * ROWS, NZ), f32),
            pltpu.VMEM((4, 1, NZ), f32),
            pltpu.VMEM((2, 4, 1, NZ), f32),
            pltpu.VMEM((3, X + 2, padded, NZ), f32),
            pltpu.VMEM((2, 2, X, NZ), f32),
            pltpu.VMEM((2, 2, X, NZ), f32),
            pltpu.VMEM((X, W, NZ), f32),
            pltpu.VMEM((X, W, NZ), f32),
            pltpu.VMEM((ni, 1, NZ), f32),
            pltpu.VMEM((ni, table, NZ), f32),
            pltpu.VMEM((ni, 4, W, NZ), f32),
            pltpu.VMEM((nd * ratio, 4, W, NZ), f32),
            dma((4,)),
            dma((STEPS, 8)),
            dma((STEPS, 8)),
            dma((4,)),
            dma((4,)),
            dma((ni,)),
            dma((ni,)),
            dma((ni,)),
            dma((nd * ratio,)),
        ],
        compiler_params=pltpu.CompilerParams(
            collective_id=0, has_side_effects=True, vmem_limit_bytes=56 << 20
        ),
    )(populations, transfer.transpose(1, 0, 2), direction)


def solution(mesh):
    in_specs = (P(None, "depth", "image", None), P("image", None, None), P("image"))
    out_specs = (
        P(None, "depth", "image", None),
        P("depth", "image", None),
        P("image", None, "depth", None),
    )
    return jax.shard_map(
        on_device, mesh=mesh, in_specs=in_specs, out_specs=out_specs, check_vma=False
    )
```

```python
import functools
import math

import jax
import jax.numpy as jnp
from jax import lax
from jax.experimental import pallas as pl
from jax.experimental.pallas import tpu as pltpu
from jax.sharding import PartitionSpec as P

STEPS = 4
MESH = pl.DeviceIdType.MESH

lattice_velocities = (
    (0, 0, 0),
    (1, 0, 0),
    (-1, 0, 0),
    (0, 1, 0),
    (0, -1, 0),
    (0, 0, 1),
    (0, 0, -1),
    (1, 1, 0),
    (-1, -1, 0),
    (1, -1, 0),
    (-1, 1, 0),
    (1, 0, 1),
    (-1, 0, -1),
    (1, 0, -1),
    (-1, 0, 1),
    (0, 1, 1),
    (0, -1, -1),
    (0, 1, -1),
    (0, -1, 1),
)
relaxation = 1.25
bump_width = 0.15
level_offset = 0.05
LOG2E = math.log2(math.e)
SCALE = math.sqrt(LOG2E) / bump_width

COUNT = len(lattice_velocities)
ORDER = (
    [n for n in range(COUNT) if lattice_velocities[n][0] == 1]
    + [n for n in range(COUNT) if lattice_velocities[n][0] == -1]
    + [n for n in range(COUNT) if lattice_velocities[n][0] == 0]
)
SLOT = {number: place for place, number in enumerate(ORDER)}
UP_Y = [n for n in range(COUNT) if lattice_velocities[n][1] == 1]
DOWN_Y = [n for n in range(COUNT) if lattice_velocities[n][1] == -1]
CROSS = len(UP_Y)
CORNERS = [n for n in range(COUNT) if lattice_velocities[n][0] and lattice_velocities[n][1]]
PAIRS = [(n, n + 1) for n in range(1, COUNT, 2)]
LOW = 8
ROWS = 8


def add_all(values):
    while len(values) > 1:
        paired = [a + b for a, b in zip(values[0::2], values[1::2])]
        values = paired + ([values[-1]] if len(values) % 2 else [])
    return values[0]


def moments(field):
    diffs = {}
    sums = [field[0]]
    for plus, minus in PAIRS:
        sums.append(field[plus] + field[minus])
        diffs[plus] = field[plus] - field[minus]
    momentum = []
    for axis in range(3):
        total = diffs[1 + 2 * axis]
        for plus, _ in PAIRS[3:]:
            factor = lattice_velocities[plus][axis]
            if factor == 1:
                total = total + diffs[plus]
            elif factor == -1:
                total = total - diffs[plus]
        momentum.append(total)
    return add_all(sums), momentum


def collide(field):
    density, momentum = moments(field)
    inverse = 1.0 / density
    square = momentum[0] * momentum[0] + momentum[1] * momentum[1] + momentum[2] * momentum[2]
    even = density - 1.5 * (square * inverse)
    keep = 1.0 - relaxation
    result = [keep * field[0] + (relaxation / 3.0) * even] + [None] * (COUNT - 1)
    parts = {}
    for divisor in (18.0, 36.0):
        parts[divisor] = ((relaxation / divisor) * even, (relaxation * 4.5 / divisor) * inverse)
    for plus, minus in PAIRS:
        project = None
        for axis in range(3):
            factor = lattice_velocities[plus][axis]
            if factor:
                if project is None:
                    project = momentum[axis]
                elif factor == 1:
                    project = project + momentum[axis]
                else:
                    project = project - momentum[axis]
        divisor = 18.0 if plus < 7 else 36.0
        base, curve = parts[divisor]
        symmetric = base + curve * (project * project)
        odd = (3.0 * relaxation / divisor) * project
        result[plus] = keep * field[plus] + (symmetric + odd)
        result[minus] = keep * field[minus] + (symmetric - odd)
    return result


def kernel(
    sizes,
    f_hbm,
    par,
    direct,
    F,
    vort,
    img,
    A,
    B,
    E,
    SY,
    RY,
    SC,
    RC,
    U,
    VS,
    VR,
    L,
    G,
    PC,
    PA,
    PS,
    PR,
    in_sem,
    halo_s,
    halo_r,
    flow_s,
    flow_r,
    pa_s,
    pa_r,
    pr_s,
    pr_r,
):
    nd, ni, X, W, NZ, bumps = sizes
    d = lax.axis_index("depth")
    i = lax.axis_index("image")
    halves = W // ROWS
    ratio = ni // nd
    chunks = 4
    step_x = X // chunks

    loads = [
        pltpu.make_async_copy(
            f_hbm.at[:, pl.ds(c * step_x, step_x)],
            F.at[:, pl.ds(c * step_x, step_x)],
            in_sem.at[c],
        )
        for c in range(chunks)
    ]
    for copy in loads:
        copy.start()

    barrier = pltpu.get_barrier_semaphore()
    everyone = nd * ni
    me = d * ni + i

    def greet(offset, carry):
        other = lax.rem(me + offset, everyone)
        pl.semaphore_signal(
            barrier,
            inc=1,
            device_id={"depth": other // ni, "image": lax.rem(other, ni)},
            device_id_type=MESH,
        )
        return carry

    lax.fori_loop(1, everyone, greet, 0)

    ray = X * nd
    lane = lax.broadcasted_iota(jnp.int32, (8, NZ), 1)
    entries = jnp.full((8, NZ), direct[0].astype(jnp.float32), jnp.float32)
    for k in range(bumps):
        for kind in range(5):
            factor = SCALE if kind == 0 else (LOG2E / ray if kind == 1 else 1.0)
            entries = jnp.where(lane == kind * bumps + k, par[kind, 0, k] * factor, entries)
    gain = pltpu.roll(entries, bumps, 1)
    shift = gain * gain - jnp.log2(entries)
    ratios = entries / gain
    for kind in (3, 4):
        ratios = jnp.where(
            lane < kind * bumps, ratios, entries / pltpu.roll(entries, (kind - 1) * bumps, 1)
        )
    table = jnp.where(lane < 2 * bumps, shift, ratios)
    table = jnp.where(lane < bumps, 2.0 * entries, table)
    PC[i] = jnp.where(lane < 5 * bumps, table, entries)[0:1]

    def to(cx, cy):
        return {"depth": lax.rem(d + cx + nd, nd), "image": lax.rem(i + cy + ni, ni)}

    def remote(src, dst, send, recv, target):
        return pltpu.make_async_remote_copy(
            src_ref=src,
            dst_ref=dst,
            send_sem=send,
            recv_sem=recv,
            device_id=target,
            device_id_type=MESH,
        )

    starts = list(range(1, W - 1 - ROWS, ROWS)) + [W - 1 - ROWS]
    edge_rows = (0, W - 1)
    outward = (DOWN_Y, UP_Y)
    inward = (UP_Y, DOWN_Y)

    def pack(b, x, start, values):
        if start == 1:
            for number in DOWN_Y:
                E[b, 0, SLOT[number], pl.ds(ROWS + x, 1), :] = values[number][0:1]
        if start == W - 1 - ROWS:
            for number in UP_Y:
                E[b, 1, SLOT[number], pl.ds(ROWS + x, 1), :] = values[number][ROWS - 1 : ROWS]

    def streamed(S, x, start):
        field = []
        for number in range(COUNT):
            cx, cy, cz = lattice_velocities[number]
            value = S[SLOT[number], x + 1 - cx, pl.ds(LOW + start - cy, ROWS), :]
            if cz:
                value = pltpu.roll(value, cz % NZ, 1)
            field.append(value)
        return field

    def edge_streamed(b, side, x):
        field = []
        for number in range(COUNT):
            cx, _, cz = lattice_velocities[number]
            rows = slice(ROWS + x - cx, 2 * ROWS + x - cx)
            if number in inward[side]:
                value = RY[b, side, inward[side].index(number), rows, :]
            else:
                value = E[b, side, SLOT[number], rows, :]
            if cz:
                value = pltpu.roll(value, cz % NZ, 1)
            field.append(value)
        return field

    def update(S, D, b, x):
        for start in starts:
            values = collide(streamed(S, x, start))
            for number in range(COUNT):
                D[SLOT[number], x + 1, pl.ds(LOW + start, ROWS), :] = values[number]
            pack(b, x, start, values)

    def put_edges(D, b, side, x, values):
        row = LOW + edge_rows[side]
        for number in range(COUNT):
            cx, cy, _ = lattice_velocities[number]
            value = values[number]
            if number in inward[side]:
                for r in range(ROWS):
                    D[SLOT[number], x + r + 1, row : row + 1, :] = value[r : r + 1]
                continue
            if cy == 0:
                E[b, side, SLOT[number], ROWS + x : 2 * ROWS + x, :] = value
            else:
                SY[side, outward[side].index(number), x : x + ROWS, :] = value
            if cx == 1 and x == X - ROWS:
                D[SLOT[number], X, row : row + 1, :] = value[ROWS - 1 : ROWS]
            if cx == -1 and x == 0:
                D[SLOT[number], 1, row : row + 1, :] = value[0:1]

    inner = pl.ds(LOW, W)

    def exchange(D, turn, columns=None):
        slot = turn % 2
        for k, number in enumerate(CORNERS):
            cx, cy, _ = lattice_velocities[number]
            side = 1 if cy == 1 else 0
            edge = X - 1 if cx == 1 else 0
            SC[k] = SY[side, outward[side].index(number), edge : edge + 1, :]
        copies = []

        def add(src, dst, target):
            k = len(copies)
            copies.append(remote(src, dst, halo_s.at[turn, k], halo_r.at[turn, k], target))
            copies[-1].start()

        body = pl.ds(ROWS, X)
        add(SY.at[1], RY.at[slot, 0, :, body], to(0, 1))
        add(SY.at[0], RY.at[slot, 1, :, body], to(0, -1))
        for k, number in enumerate(CORNERS):
            cx, cy, _ = lattice_velocities[number]
            add(SC.at[k], RC.at[slot, k], to(cx, cy))
        if columns is not None:
            for x in (0, X - 1):
                columns(x, 0)
        add(D.at[pl.ds(0, CROSS), X, inner], D.at[pl.ds(0, CROSS), 0, inner], to(1, 0))
        add(D.at[pl.ds(CROSS, CROSS), 1, inner], D.at[pl.ds(CROSS, CROSS), X + 1, inner], to(-1, 0))
        return copies

    def finish(copies, D, turn):
        slot = turn % 2
        for copy in copies:
            copy.wait()
        for number in range(COUNT):
            cx, cy, _ = lattice_velocities[number]
            if cx == 0:
                continue
            plane, place = (0, ROWS - 1) if cx == 1 else (X + 1, ROWS + X)
            for side in range(2):
                if number in inward[side]:
                    k = CORNERS.index(number)
                    j = inward[side].index(number)
                    RY[slot, side, j, place : place + 1, :] = RC[slot, k]
                else:
                    row = LOW + edge_rows[side] - cy
                    E[slot, side, SLOT[number], place : place + 1, :] = D[
                        SLOT[number], plane, row : row + 1, :
                    ]

    def first(x, carry):
        for h in range(halves):
            field = [F[number, x, pl.ds(ROWS * h, ROWS), :] for number in range(COUNT)]
            values = collide(field)
            for number in range(COUNT):
                A[SLOT[number], x + 1, pl.ds(LOW + ROWS * h, ROWS), :] = values[number]
            for side, edge in ((0, 0), (1, ROWS - 1)):
                if h != (0 if side == 0 else halves - 1):
                    continue
                near = 1 if side == 0 else ROWS - 2
                for number in range(COUNT):
                    if lattice_velocities[number][1] == 0:
                        E[0, side, SLOT[number], pl.ds(ROWS + x, 1), :] = values[number][
                            edge : edge + 1
                        ]
                for j, number in enumerate(outward[side]):
                    SY[side, j, pl.ds(x, 1), :] = values[number][edge : edge + 1]
                    E[0, side, SLOT[number], pl.ds(ROWS + x, 1), :] = values[number][
                        near : near + 1
                    ]
        return carry

    for c in range(chunks):
        loads[c].wait()
        lax.fori_loop(c * step_x, (c + 1) * step_x, first, 0)

    pl.semaphore_wait(barrier, everyone - 1)
    shares = [
        remote(PC.at[i], PC.at[i], pa_s.at[o], pa_r.at[o], to(0, o)) for o in range(1, ni)
    ]
    copies = exchange(A, 0)
    for copy in shares:
        copy.start()

    source, target = A, B
    for turn in range(1, STEPS):

        def middle(x, carry, source=source, target=target, turn=turn):
            update(source, target, turn % 2, x)
            return carry

        lax.fori_loop(1, X - 1, middle, 0)
        finish(copies, source, turn - 1)
        for side in range(2):
            for x in range(0, X, ROWS):
                put_edges(target, turn % 2, side, x, collide(edge_streamed((turn - 1) % 2, side, x)))
        copies = exchange(target, turn, middle)
        source, target = target, source

    def flow_of(field):
        density, momentum = moments(field)
        inverse = 1.0 / density
        return [momentum[axis] * inverse for axis in (1, 2, 0)]

    def last(x, carry):
        for start in starts:
            field = streamed(source, x, start)
            for number in range(COUNT):
                F[number, x, pl.ds(start, ROWS), :] = field[number]
            for place, value in enumerate(flow_of(field)):
                U[place, x + 1, pl.ds(LOW + start, ROWS), :] = value
        return carry

    lax.fori_loop(1, X - 1, last, 0)
    finish(copies, source, STEPS - 1)
    for x in (0, X - 1):
        last(x, 0)
    for side in range(2):
        row = edge_rows[side]
        for x in range(0, X, ROWS):
            field = edge_streamed((STEPS - 1) % 2, side, x)
            flow = flow_of(field)
            for place, value in enumerate(flow):
                for r in range(ROWS):
                    U[place, x + r + 1, LOW + row : LOW + row + 1, :] = value[r : r + 1]
            VS[side, 0, x : x + ROWS, :] = flow[1]
            VS[side, 1, x : x + ROWS, :] = flow[2]
    flows = [
        remote(VS.at[1], VR.at[1], flow_s.at[0], flow_r.at[0], to(0, 1)),
        remote(VS.at[0], VR.at[0], flow_s.at[1], flow_r.at[1], to(0, -1)),
        remote(
            U.at[pl.ds(0, 2), X, inner],
            U.at[pl.ds(0, 2), 0, inner],
            flow_s.at[2],
            flow_r.at[2],
            to(1, 0),
        ),
        remote(
            U.at[pl.ds(0, 2), 1, inner],
            U.at[pl.ds(0, 2), X + 1, inner],
            flow_s.at[3],
            flow_r.at[3],
            to(-1, 0),
        ),
    ]
    for copy in flows:
        copy.start()
    for side in range(2):
        row = edge_rows[side]
        for x in range(0, X, ROWS):
            field = edge_streamed((STEPS - 1) % 2, side, x)
            for number in range(COUNT):
                for r in range(ROWS):
                    F[number, x + r, row : row + 1, :] = field[number][r : r + 1]
    for copy in shares:
        copy.wait()

    def expand(m, carry):
        for block in range(PA.shape[1] // 8):
            line = lax.broadcasted_iota(jnp.int32, (8, NZ), 0) + 8 * block
            chosen = jnp.where(lane == line, jnp.broadcast_to(PC[m], (8, NZ)), 0.0)
            value = jnp.sum(chosen, axis=1, keepdims=True)
            PA[m, pl.ds(8 * block, 8), :] = jnp.broadcast_to(value, (8, NZ))
        return carry

    lax.fori_loop(0, ni, expand, 0, unroll=2)
    for copy in flows:
        copy.wait()

    def flow_rows(x, carry):
        for place, j in ((1, 0), (2, 1)):
            U[place, x + 1, pl.ds(LOW - 1, 1), :] = VR[1, j, pl.ds(x, 1), :]
            U[place, x + 1, pl.ds(LOW + W, 1), :] = VR[0, j, pl.ds(x, 1), :]
        return carry

    lax.fori_loop(0, X, flow_rows, 0)

    def spin(x, carry):
        def across_x(place):
            return (U[place, x + 2, inner, :] - U[place, x, inner, :]) * 0.5

        def across_y(place):
            above = U[place, x + 1, pl.ds(LOW + 1, W), :]
            return (above - U[place, x + 1, pl.ds(LOW - 1, W), :]) * 0.5

        def across_z(place):
            value = U[place, x + 1, inner, :]
            return (pltpu.roll(value, NZ - 1, 1) - pltpu.roll(value, 1, 1)) * 0.5

        spin_x = across_y(1) - across_z(0)
        spin_y = across_z(2) - across_x(1)
        spin_z = across_x(0) - across_y(2)
        size = jnp.sqrt(spin_x * spin_x + spin_y * spin_y + spin_z * spin_z)
        rounded = size.astype(jnp.bfloat16)
        vort[x] = rounded
        value = rounded.astype(jnp.float32)
        level = (value / (value + level_offset)) * SCALE
        L[x] = level
        G[x] = jnp.exp2(-(level * level))
        return carry

    lax.fori_loop(0, X, spin, 0, unroll=2)

    owner = i // ratio
    mine = d * ratio + lax.rem(i, ratio)

    def row(m, r):
        return jnp.broadcast_to(PA[m, pl.ds(r, 1), :], (ROWS, NZ))

    def blend(backward, through, colors, local_through, local_colors):
        fade = jnp.where(backward, local_through, 1.0)
        lit = jnp.where(backward, 1.0, through)
        mixed = [color * fade + lit * local for color, local in zip(colors, local_colors)]
        return through * local_through, mixed

    def piece(o, m):
        return remote(
            PS.at[m],
            PR.at[mine],
            pr_s.at[o],
            pr_r.at[mine],
            {"depth": owner, "image": m},
        )

    def render(o, carry):
        m = lax.rem(i + 1 + o, ni)
        backward = row(m, 5 * bumps) > 0.5

        def along(x, state):
            new = []
            levels = [L[x, pl.ds(ROWS * h, ROWS), :] for h in range(halves)]
            totals = [[None] * 4 for h in range(halves)]
            for k in range(bumps):
                centre = row(m, k)
                shift = row(m, bumps + k)
                gains = [row(m, (1 + j) * bumps + k) for j in range(1, 4)]
                for h in range(halves):
                    bump = jnp.exp2(levels[h] * centre - shift)
                    for j in range(4):
                        term = gains[j - 1] * bump if j else bump
                        totals[h][j] = term if k == 0 else totals[h][j] + term
            for h in range(halves):
                through, colors = state[4 * h], state[4 * h + 1 : 4 * h + 4]
                common = G[x, pl.ds(ROWS * h, ROWS), :]
                optical = totals[h][0] * common
                local = jnp.exp2(-optical)
                alpha = (1.0 - local) * common
                shades = [alpha * total for total in totals[h][1:]]
                through, colors = blend(backward, through, colors, local, shades)
                new += [through] + list(colors)
            return tuple(new)

        zero = jnp.zeros((ROWS, NZ), jnp.float32)
        start = (jnp.ones((ROWS, NZ), jnp.float32), zero, zero, zero) * halves
        state = lax.fori_loop(0, X, along, start, unroll=2)
        for h in range(halves):
            through, colors = state[4 * h], state[4 * h + 1 : 4 * h + 4]
            for j, value in enumerate(list(colors) + [through]):
                PS[m, j, pl.ds(ROWS * h, ROWS), :] = value
        local_target = jnp.logical_and(owner == d, m == i)

        @pl.when(local_target)
        def _():
            PR[mine] = PS[m]

        @pl.when(jnp.logical_not(local_target))
        def _():
            piece(o, m).start()

        return carry

    lax.fori_loop(0, ni, render, 0)

    def sent(o, carry):
        m = lax.rem(i + 1 + o, ni)

        @pl.when(jnp.logical_not(jnp.logical_and(owner == d, m == i)))
        def _():
            piece(o, m).wait_send()

        return carry

    def arrived(slot, carry):
        @pl.when(jnp.logical_not(jnp.logical_and(owner == d, slot == mine)))
        def _():
            remote(
                PS.at[0], PR.at[slot], pr_s.at[0], pr_r.at[slot], {"depth": d, "image": i}
            ).wait_recv()

        return carry

    lax.fori_loop(0, nd * ratio, arrived, 0)
    backward = row(i, 5 * bumps) > 0.5
    for part in range(ratio):
        for h in range(halves):
            rows = pl.ds(ROWS * h, ROWS)
            through = jnp.ones((ROWS, NZ), jnp.float32)
            colors = [jnp.zeros((ROWS, NZ), jnp.float32)] * 3
            for slab in range(nd):
                slot = slab * ratio + part
                local = [PR[slot, j, rows, :] for j in range(4)]
                through, colors = blend(backward, through, colors, local[3], local[:3])
            for j, value in enumerate(colors + [1.0 - through]):
                img[0, j, pl.ds(part * W + ROWS * h, ROWS), :] = value
    lax.fori_loop(0, ni, sent, 0)


def on_device(populations, transfer, direction):
    nd, ni = lax.axis_size("depth"), lax.axis_size("image")
    count, X, W, NZ = populations.shape
    bumps = transfer.shape[2]
    assert transfer.shape[0] == 1 and ni % nd == 0 and W % ROWS == 0 and W >= 2 * ROWS and X % 8 == 0
    sizes = (nd, ni, X, W, NZ, bumps)
    ratio = ni // nd
    padded = W + 2 * ROWS
    f32 = jnp.float32
    table = -(-(5 * bumps + 1) // 8) * 8
    dma = pltpu.SemaphoreType.DMA
    return pl.pallas_call(
        functools.partial(kernel, sizes),
        out_shape=(
            pltpu.VMEM(populations.shape, f32),
            jax.ShapeDtypeStruct((X, W, NZ), jnp.bfloat16),
            jax.ShapeDtypeStruct((1, 4, ratio * W, NZ), f32),
        ),
        in_specs=[
            pl.BlockSpec(memory_space=pl.ANY),
            pl.BlockSpec(memory_space=pltpu.SMEM),
            pl.BlockSpec(memory_space=pltpu.SMEM),
        ],
        out_specs=(
            pl.BlockSpec(memory_space=pltpu.VMEM),
            pl.BlockSpec(memory_space=pltpu.VMEM),
            pl.BlockSpec(memory_space=pltpu.VMEM),
        ),
        scratch_shapes=[
            pltpu.VMEM((COUNT, X + 2, padded, NZ), f32),
            pltpu.VMEM((COUNT, X + 2, padded, NZ), f32),
            pltpu.VMEM((2, 2, COUNT, X + 2 * ROWS, NZ), f32),
            pltpu.VMEM((2, CROSS, X, NZ), f32),
            pltpu.VMEM((2, 2, CROSS, X + 2 * ROWS, NZ), f32),
            pltpu.VMEM((4, 1, NZ), f32),
            pltpu.VMEM((2, 4, 1, NZ), f32),
            pltpu.VMEM((3, X + 2, padded, NZ), f32),
            pltpu.VMEM((2, 2, X, NZ), f32),
            pltpu.VMEM((2, 2, X, NZ), f32),
            pltpu.VMEM((X, W, NZ), f32),
            pltpu.VMEM((X, W, NZ), f32),
            pltpu.VMEM((ni, 1, NZ), f32),
            pltpu.VMEM((ni, table, NZ), f32),
            pltpu.VMEM((ni, 4, W, NZ), f32),
            pltpu.VMEM((nd * ratio, 4, W, NZ), f32),
            dma((4,)),
            dma((STEPS, 8)),
            dma((STEPS, 8)),
            dma((4,)),
            dma((4,)),
            dma((ni,)),
            dma((ni,)),
            dma((ni,)),
            dma((nd * ratio,)),
        ],
        compiler_params=pltpu.CompilerParams(
            collective_id=0, has_side_effects=True, vmem_limit_bytes=56 << 20
        ),
    )(populations, transfer.transpose(1, 0, 2), direction)


def solution(mesh):
    in_specs = (P(None, "depth", "image", None), P("image", None, None), P("image"))
    out_specs = (
        P(None, "depth", "image", None),
        P("depth", "image", None),
        P("image", None, "depth", None),
    )
    return jax.shard_map(
        on_device, mesh=mesh, in_specs=in_specs, out_specs=out_specs, check_vma=False
    )
```
